256 devices in a mesh: region: 64 (over x, z, core), step: 4 (over y).
Axes of the slice: x: 4, y: 4, z: 8, core: 2. Of those that a mesh axis runs over, the one named last changes fastest.
Arguments:
- features: bfloat16 [4096, 64, 256], P('region', 'step'), may hold values from -6 to 6
- neighbours: int32 [4096, 32], P('region'), may hold values from 0 to 4095, as said below
- polylines: bfloat16 [16384, 256], P('region'), may hold values from -6 to 6
- temporal_gain: float32 [256], replicated, may hold values from 0.5 to 6
- social_gain: float32 [256], replicated, may hold values from 0.5 to 6
- map_gain: float32 [256], replicated, may hold values from 0.5 to 6
- ffn_gain: float32 [256], replicated, may hold values from 0.5 to 1.5
- temporal_weights: bfloat16 [4, 256, 256], replicated, may hold values from -0.375 to 0.375
- social_weights: bfloat16 [4, 256, 256], replicated, may hold values from -0.375 to 0.375
- map_weights: bfloat16 [4, 256, 256], replicated, may hold values from -0.375 to 0.375
- ffn_up: bfloat16 [256, 1024], replicated, may hold values from -0.375 to 0.375
- ffn_down: bfloat16 [1024, 256], replicated, may hold values from -0.1875 to 0.1875
Outputs:
- encoded: bfloat16 [4096, 64, 256], P('region', 'step')
The draws below stay inside these ranges and needn't reach their ends.
Inputs may be any that keep to these rules, and one draw needn't show every extreme that they name: `neighbours`: each agent's 32 entries are distinct ids of other agents, of its own region or of a neighbour region on the grid.
All inputs are finite; a program needn't handle non-finite values.
Results may differ from the reference program's by a relative error of at most 0.035.
The reference program's roundings to bfloat16 on the way count: a program that leaves them out, or rounds other values in their place, can miss the bound.
Values may be sent and summed in bfloat16 or wider, within the bound.
A program may use at most 128 MiB of HBM per device.

```python
import jax
import jax.numpy as jnp
from jax import lax

D = 256
HEADS = 8
HEAD_DIM = 32
FF = 1024
A_DEV = 64
STEPS = 64
NBR = 32
P_DEV = 256
GRID_W = 4
AGENTS = 4096
POLYS = 16384
N_REGION = 64


def norm_gain(key, salt):
    folded = jax.random.fold_in(key, salt)
    return jax.random.uniform(folded, (D,), jnp.float32, 0.5, 1.5)


def draw_temporal_gain(key, part):
    return norm_gain(key, 11)


def draw_social_gain(key, part):
    return norm_gain(key, 23)


def draw_map_gain(key, part):
    return norm_gain(key, 37)


def draw_neighbours(key, part):
    regions = AGENTS // A_DEV
    agent = jnp.arange(AGENTS, dtype=jnp.int32)
    region = agent // A_DEV
    column = region % GRID_W
    offsets = jnp.array([0, -1, 1, -GRID_W, GRID_W], jnp.int32)
    source = region[:, None] + offsets[None, :]
    usable = (source >= 0) & (source < regions)
    usable = usable & jnp.logical_not((offsets[None, :] == -1) & (column[:, None] == 0))
    usable = usable & jnp.logical_not((offsets[None, :] == 1) & (column[:, None] == GRID_W - 1))
    slots = jnp.arange(A_DEV, dtype=jnp.int32)
    candidate = (source[:, :, None] * A_DEV + slots[None, None, :]).reshape(AGENTS, 5 * A_DEV)
    usable = jnp.repeat(usable, A_DEV, axis=1) & (candidate != agent[:, None])
    noise = jax.random.randint(jax.random.fold_in(key, 5), (AGENTS, 5 * A_DEV), 0, 2 ** 19)
    order = jnp.arange(5 * A_DEV, dtype=jnp.int32)
    score = jnp.where(usable, noise * 2048 + order[None, :], -1)
    picked = lax.top_k(score, NBR)[1]
    return jnp.take_along_axis(candidate, picked, axis=1).astype(jnp.int32)


def shard_levels(rng, dims, split, least, largest):
    def one(dim, parts):
        heights = jax.random.uniform(jax.random.fold_in(jax.random.fold_in(rng, 6), dim), (parts,), jnp.float32, least / len(split), largest / len(split))
        return jnp.repeat(jnp.exp(heights), dims[dim] // parts).reshape((-1,) + (1,) * (len(dims) - dim - 1))

    level = one(*split[0])
    for cut in split[1:]:
        level = level * one(*cut)
    return level


def scatter_about(rng, shape, width, most, pieces=(), held_as=jnp.bfloat16):
    result = jax.random.normal(rng, shape, jnp.float32) * width
    if len(pieces) > 0:
        result = shard_levels(rng, shape, pieces, -0.22, 0.18) * result
    return jnp.clip(result, min=-most, max=most).astype(held_as)


def setup_inputs(seed: int = 0) -> dict:
    streams_of = jax.random.split(jax.random.key(seed), 13)
    return {
        "features": scatter_about(streams_of[0], (AGENTS, STEPS, D), 1.0, 6.0, ((0, 64), (1, 4))),
        "neighbours": draw_neighbours(jax.random.fold_in(streams_of[12], 71), 0),
        "polylines": scatter_about(streams_of[2], (POLYS, D), 1.0, 6.0, ((0, 64),)),
        "temporal_gain": draw_temporal_gain(jax.random.fold_in(streams_of[12], 71), 0),
        "social_gain": draw_social_gain(jax.random.fold_in(streams_of[12], 71), 0),
        "map_gain": draw_map_gain(jax.random.fold_in(streams_of[12], 71), 0),
        "ffn_gain": jnp.clip(1.0 + 0.1 * jax.random.normal(streams_of[6], (D,), jnp.float32), 0.5, 1.5),
        "temporal_weights": scatter_about(streams_of[7], (4, D, D), D ** -0.5, 0.375),
        "social_weights": scatter_about(streams_of[8], (4, D, D), D ** -0.5, 0.375),
        "map_weights": scatter_about(streams_of[9], (4, D, D), D ** -0.5, 0.375),
        "ffn_up": scatter_about(streams_of[10], (D, FF), D ** -0.5, 0.375),
        "ffn_down": scatter_about(streams_of[11], (FF, D), FF ** -0.5, 0.1875),
    }


def normed(x, gain):
    xf = x.astype(jnp.float32)
    inv = lax.rsqrt(lax.optimization_barrier(jnp.mean(xf * xf, axis=-1, keepdims=True)) + 1e-06)
    return (xf * inv * gain.astype(jnp.float32)).astype(jnp.bfloat16)

def project(rows, weight):
    flat = rows.reshape(-1, rows.shape[-1])
    out = jnp.dot(flat, weight, preferred_element_type=jnp.float32)
    return out.reshape(rows.shape[:-1] + (weight.shape[1],))

def probs_of(scores):
    top = lax.optimization_barrier(jnp.max(scores, axis=-1, keepdims=True))
    expo = jnp.exp(scores - top)
    return (expo / lax.optimization_barrier(jnp.sum(expo, axis=-1, keepdims=True))).astype(jnp.bfloat16)

def reference(features, neighbours, polylines, temporal_gain, social_gain, map_gain, ffn_gain, temporal_weights, social_weights, map_weights, ffn_up, ffn_down):
    scale = HEAD_DIM ** (-0.5)
    f32 = jnp.float32
    bf16 = jnp.bfloat16
    n1 = normed(features, temporal_gain)
    q1 = project(n1, temporal_weights[0]).astype(bf16).reshape(N_REGION, A_DEV, STEPS, HEADS, HEAD_DIM)
    k1 = project(n1, temporal_weights[1]).astype(bf16).reshape(N_REGION, A_DEV, STEPS, HEADS, HEAD_DIM)
    v1 = project(n1, temporal_weights[2]).astype(bf16).reshape(N_REGION, A_DEV, STEPS, HEADS, HEAD_DIM)

    def temporal_block(items):
        query, keys, values = items
        scores = jnp.einsum('athd,ashd->ahts', query.astype(f32), keys.astype(f32)) * scale
        probs = probs_of(scores)
        return jnp.einsum('ahts,ashd->athd', probs.astype(f32), values.astype(f32)).astype(bf16)
    o1 = lax.map(temporal_block, (q1, k1, v1)).reshape(AGENTS, STEPS, D)
    after1 = (features.astype(f32) + project(o1, temporal_weights[3])).astype(bf16)
    n2 = normed(after1, social_gain)
    q2 = project(n2, social_weights[0]).astype(bf16).reshape(N_REGION, A_DEV, STEPS, HEADS, HEAD_DIM)
    k2 = project(n2, social_weights[1]).astype(bf16)
    v2 = project(n2, social_weights[2]).astype(bf16)
    k2_blocks = k2.reshape(N_REGION, A_DEV, STEPS, D)
    v2_blocks = v2.reshape(N_REGION, A_DEV, STEPS, D)
    nbr_blocks = neighbours.reshape(N_REGION, A_DEV, NBR)

    def social_block(items):
        query, own_k, own_v, ids = items
        keys = jnp.concatenate([own_k[:, None], jnp.take(k2, ids, axis=0)], axis=1)
        values = jnp.concatenate([own_v[:, None], jnp.take(v2, ids, axis=0)], axis=1)
        keys = keys.reshape(A_DEV, NBR + 1, STEPS, HEADS, HEAD_DIM).astype(f32)
        values = values.reshape(A_DEV, NBR + 1, STEPS, HEADS, HEAD_DIM).astype(f32)
        scores = jnp.einsum('athd,anthd->athn', query.astype(f32), keys) * scale
        probs = probs_of(scores)
        return jnp.einsum('athn,anthd->athd', probs.astype(f32), values).astype(bf16)
    o2 = lax.map(social_block, (q2, k2_blocks, v2_blocks, nbr_blocks)).reshape(AGENTS, STEPS, D)
    after2 = (after1.astype(f32) + project(o2, social_weights[3])).astype(bf16)
    n3 = normed(after2, map_gain)
    q3 = project(n3, map_weights[0]).astype(bf16).reshape(N_REGION, A_DEV * STEPS, HEADS, HEAD_DIM)
    kp = project(polylines, map_weights[1]).astype(bf16).reshape(N_REGION, P_DEV, D)
    vp = project(polylines, map_weights[2]).astype(bf16).reshape(N_REGION, P_DEV, D)
    offsets = jnp.array([0, -1, 1, -GRID_W, GRID_W], jnp.int32)

    def map_block(items):
        region, query = items
        column = region % GRID_W
        sources = region + offsets
        exists = jnp.stack([region >= 0, column != 0, column != GRID_W - 1, region >= GRID_W, region < N_REGION - GRID_W])
        index = jnp.clip(sources, 0, N_REGION - 1).astype(jnp.int32)
        keys = jnp.take(kp, index, axis=0).reshape(5 * P_DEV, HEADS, HEAD_DIM).astype(f32)
        values = jnp.take(vp, index, axis=0).reshape(5 * P_DEV, HEADS, HEAD_DIM).astype(f32)
        allowed = jnp.repeat(exists, P_DEV)
        scores = jnp.einsum('rhd,phd->hrp', query.astype(f32), keys) * scale
        scores = jnp.where(allowed[None, None, :], scores, -jnp.inf)
        probs = probs_of(scores)
        return jnp.einsum('hrp,phd->rhd', probs.astype(f32), values).astype(bf16)
    regions = jnp.arange(N_REGION, dtype=jnp.int32)
    o3 = lax.map(map_block, (regions, q3)).reshape(AGENTS, STEPS, D)
    after3 = (after2.astype(f32) + project(o3, map_weights[3])).astype(bf16)
    n4 = normed(after3, ffn_gain)
    hidden = jax.nn.gelu(project(n4, ffn_up), approximate=True).astype(bf16)
    return (after3.astype(f32) + project(hidden, ffn_down)).astype(bf16)
```

```python
import functools
import math

import jax
import jax.numpy as jnp
from jax import lax
from jax.experimental import pallas as pl
from jax.experimental.pallas import tpu as pltpu
from jax.sharding import PartitionSpec as P

HEADS = 8
HEAD_DIM = 32
GRID_W = 4
BF16 = jnp.bfloat16
F32 = jnp.float32
QSCALE = HEAD_DIM ** (-0.5) * math.log2(math.e)
OPPOSITE = (0, 2, 1, 4, 3)
MESH = pl.DeviceIdType.MESH


def dot(a, b):
    return jnp.dot(a, b, preferred_element_type=F32)


def dot_nt(a, b):
    return lax.dot_general(a, b, (((1,), (1,)), ((), ())), preferred_element_type=F32)


def normed(x, gain):
    xf = x.astype(F32)
    inv = lax.rsqrt(jnp.mean(xf * xf, axis=-1, keepdims=True) + 1e-06)
    return (xf * inv * gain).astype(BF16)


def small_attention(q, keys, values, head_rows, bias=None):
    rows, width = q.shape
    stacked = jnp.concatenate([q * head_rows[h : h + 1].astype(BF16) for h in range(HEADS)], axis=0)
    scores = dot_nt(stacked, keys)
    if bias is not None:
        scores = (scores.reshape(HEADS, rows, -1) + bias[None]).reshape(HEADS * rows, -1)
    top = jnp.max(scores, axis=-1, keepdims=True)
    expo = jnp.exp2(scores - top)
    total = jnp.sum(expo, axis=-1, keepdims=True)
    out = dot(expo.astype(BF16), values)
    num = out[0:rows]
    den = jnp.broadcast_to(total[0:rows], (rows, width))
    for h in range(1, HEADS):
        here = head_rows[h : h + 1] > 0.5
        num = jnp.where(here, out[h * rows : (h + 1) * rows], num)
        den = jnp.where(here, total[h * rows : (h + 1) * rows], den)
    return (num / den).astype(BF16)


def kernel(
    n_region, ny, chunks,
    feat, nbr, poly, g1, g2, g3, g4, tw, sw, mw, fu, fd,
    out,
    fall, qkv, o1, back, cand, polys, kpt, rhs, k2, v2, enc, twv, swv, mwv, fuv, fdv,
    own_sem, w_sem, a_send, a_recv, p_send, p_recv, b_send, b_recv, h_send, h_recv,
):
    region = lax.axis_index("region")
    step = lax.axis_index("step")
    column = lax.rem(region, GRID_W)
    exists = (None, column != 0, column != GRID_W - 1, region >= GRID_W, region < n_region - GRID_W)
    others = (region, region - 1, region + 1, region - GRID_W, region + GRID_W)
    ac, steps = fall.shape[1], fall.shape[2]
    agents, width = cand.shape[2], cand.shape[3]
    tc = steps // chunks
    rows = tc * agents
    block = ac * steps

    barrier = pltpu.get_barrier_semaphore()
    peers = [lax.rem(step + d, ny) for d in range(1, ny)]
    for peer in peers:
        pl.semaphore_signal(barrier, inc=1, device_id=(region, peer), device_id_type=MESH)
    for k in range(1, 5):
        @pl.when(exists[k])
        def _():
            pl.semaphore_signal(barrier, inc=1, device_id=(others[k], step), device_id_type=MESH)

    def own_copy():
        return pltpu.make_async_copy(
            feat.at[pl.ds(pl.multiple_of(step * ac, ac), ac)], fall.at[step], own_sem.at[0]
        )

    def poly_copy():
        return pltpu.make_async_copy(poly, polys.at[0], own_sem.at[1])

    weights = ((tw, twv), (sw, swv), (mw, mwv), (fu, fuv), (fd, fdv))

    def weight_copy(i):
        return pltpu.make_async_copy(weights[i][0], weights[i][1], w_sem.at[i])

    own_copy().start()
    poly_copy().start()
    for i in range(5):
        weight_copy(i).start()

    greeted = ny - 1
    for k in range(1, 5):
        greeted = greeted + exists[k].astype(jnp.int32)
    pl.semaphore_wait(barrier, greeted)

    def a_copy(d):
        peer = peers[d - 1]
        return pltpu.make_async_remote_copy(
            src_ref=feat.at[pl.ds(pl.multiple_of(peer * ac, ac), ac)],
            dst_ref=fall.at[step],
            send_sem=a_send.at[d - 1],
            recv_sem=a_recv.at[d - 1],
            device_id=(region, peer),
            device_id_type=MESH,
        )

    def p_copy(k):
        return pltpu.make_async_remote_copy(
            src_ref=poly,
            dst_ref=polys.at[OPPOSITE[k]],
            send_sem=p_send.at[k - 1],
            recv_sem=p_recv.at[OPPOSITE[k] - 1],
            device_id=(others[k], step),
            device_id_type=MESH,
        )

    def b_copy(d, c):
        peer = peers[d - 1]
        return pltpu.make_async_remote_copy(
            src_ref=back.at[peer, pl.ds(c * tc, tc)],
            dst_ref=cand.at[0, pl.ds(c * tc, tc), pl.ds(pl.multiple_of(step * ac, ac), ac)],
            send_sem=b_send.at[d - 1, c],
            recv_sem=b_recv.at[d - 1, c],
            device_id=(region, peer),
            device_id_type=MESH,
        )

    def h_copy(k, c):
        return pltpu.make_async_remote_copy(
            src_ref=cand.at[0, pl.ds(c * tc, tc)],
            dst_ref=cand.at[OPPOSITE[k], pl.ds(c * tc, tc)],
            send_sem=h_send.at[k - 1, c],
            recv_sem=h_recv.at[OPPOSITE[k] - 1, c],
            device_id=(others[k], step),
            device_id_type=MESH,
        )

    def h_arrival(k, c):
        return pltpu.make_async_remote_copy(
            src_ref=cand.at[0, pl.ds(c * tc, tc)],
            dst_ref=cand.at[k, pl.ds(c * tc, tc)],
            send_sem=h_send.at[k - 1, c],
            recv_sem=h_recv.at[k - 1, c],
            device_id=(others[k], step),
            device_id_type=MESH,
        )

    def p_arrival(k):
        return pltpu.make_async_remote_copy(
            src_ref=poly,
            dst_ref=polys.at[k],
            send_sem=p_send.at[k - 1],
            recv_sem=p_recv.at[k - 1],
            device_id=(others[k], step),
            device_id_type=MESH,
        )

    for d in range(1, ny):
        a_copy(d).start()
    for k in range(1, 5):
        @pl.when(exists[k])
        def _():
            p_copy(k).start()

    head_rows = (
        lax.broadcasted_iota(jnp.int32, (HEADS, width), 1) // HEAD_DIM
        == lax.broadcasted_iota(jnp.int32, (HEADS, width), 0)
    ).astype(F32)
    row_i = lax.broadcasted_iota(jnp.int32, (block, block), 0)
    col_j = lax.broadcasted_iota(jnp.int32, (block, block), 1)
    to_steps = (col_j == lax.rem(row_i, ac) * steps + row_i // ac).astype(F32).astype(BF16)
    to_agents = (col_j == lax.rem(row_i, steps) * ac + row_i // steps).astype(F32).astype(BF16)

    slot = lax.broadcasted_iota(jnp.int32, (1, agents), 1)
    ids = jnp.concatenate([other * agents + slot for other in others], axis=1)
    self_id = region * agents + lax.broadcasted_iota(jnp.int32, (agents, 1), 0)
    linked = (self_id == ids).astype(F32)
    for n in range(nbr.shape[1]):
        linked = jnp.where(nbr[:, n : n + 1] == ids, 1.0, linked)
    bias = jnp.where(linked > 0.5, 0.0, -1e30)

    own_copy().wait()
    weight_copy(0).wait()
    for d in range(1, ny):
        a_copy(d).wait()
    for y in range(ny):
        n1 = normed(fall[y].reshape(block, width), g1[...])
        qkv[y, :, :, 0:width] = (dot(n1, twv[0]) * QSCALE).astype(BF16).reshape(ac, steps, width)
        qkv[y, :, :, width : 2 * width] = dot(n1, twv[1]).astype(BF16).reshape(ac, steps, width)
        qkv[y, :, :, 2 * width : 3 * width] = dot(n1, twv[2]).astype(BF16).reshape(ac, steps, width)

    def one_agent(a, carry):
        every = ny * steps
        q = qkv[:, a, :, 0:width].reshape(every, width)
        keys = qkv[:, a, :, width : 2 * width].reshape(every, width)
        values = qkv[:, a, :, 2 * width : 3 * width].reshape(every, width)
        mixed = small_attention(q, keys, values, head_rows)
        o1[:, a] = mixed.reshape(ny, steps, width)
        return carry

    lax.fori_loop(0, ac, one_agent, 0)
    for y in range(ny):
        after1 = fall[y].reshape(block, width).astype(F32) + dot(o1[y].reshape(block, width), twv[3])
        back[y] = dot(to_steps, after1.astype(BF16)).astype(BF16).reshape(steps, ac, width)

    for c in range(chunks):
        for d in range(1, ny):
            b_copy(d, c).start()

    mine = pltpu.make_async_copy(
        back.at[step], cand.at[0, :, pl.ds(pl.multiple_of(step * ac, ac), ac)], own_sem.at[0]
    )
    mine.start()

    poly_copy().wait()
    weight_copy(2).wait()
    for k in range(1, 5):
        @pl.when(exists[k])
        def _():
            p_arrival(k).wait_recv()

        @pl.when(jnp.logical_not(exists[k]))
        def _():
            polys[k] = polys[0]
            cand[k] = jnp.zeros_like(cand[k])
    count = polys.shape[1]
    for k in range(5):
        keys = dot(polys[k], mwv[1])
        kpt[:, k * count : (k + 1) * count] = keys.T.astype(BF16)
        values = dot(polys[k], mwv[2])
        valid = 1.0 if k == 0 else jnp.where(exists[k], 1.0, 0.0)
        for h in range(HEADS):
            ext = jnp.where(head_rows[h : h + 1] > 0.5, values, 1.0)
            rhs[h, k * count : (k + 1) * count] = (ext * valid).astype(BF16)

    mine.wait()
    for c in range(chunks):
        for d in range(1, ny):
            b_copy(d, c).wait_recv()
        for k in range(1, 5):
            @pl.when(exists[k])
            def _():
                h_copy(k, c).start()
    for i in (1, 3, 4):
        weight_copy(i).wait()

    def one_chunk(c, carry):
        for k in range(1, 5):
            @pl.when(exists[k])
            def _():
                h_arrival(k, c).wait_recv()
        part = pl.ds(c * tc, tc)
        for k in range(5):
            n2 = normed(cand[k, part].reshape(rows, width), g2[...])
            k2[k] = dot(n2, swv[1]).astype(BF16).reshape(tc, agents, width)
            v2[k] = dot(n2, swv[2]).astype(BF16).reshape(tc, agents, width)
            if k == 0:
                q2 = (dot(n2, swv[0]) * QSCALE).astype(BF16)
        mixes = []
        for t in range(tc):
            keys = k2[:, t].reshape(5 * agents, width)
            values = v2[:, t].reshape(5 * agents, width)
            mixes.append(
                small_attention(q2[t * agents : (t + 1) * agents], keys, values, head_rows, bias)
            )
        o2 = jnp.concatenate(mixes, axis=0)
        after2 = (cand[0, part].reshape(rows, width).astype(F32) + dot(o2, swv[3])).astype(BF16)
        n3 = normed(after2, g3[...])
        q3 = (dot(n3, mwv[0]) * QSCALE).astype(BF16)
        num = jnp.zeros((rows, width), F32)
        den = jnp.zeros((rows, width), F32)
        for h in range(HEADS):
            scores = dot(q3 * head_rows[h : h + 1].astype(BF16), kpt[...])
            top = jnp.max(scores, axis=-1, keepdims=True)
            expo = jnp.exp2(scores - top).astype(BF16)
            both = dot(expo, rhs[h])
            after = (h + 1) % HEADS
            num = jnp.where(head_rows[h : h + 1] > 0.5, both, num)
            den = jnp.where(head_rows[after : after + 1] > 0.5, both, den)
        den = pltpu.roll(den, width - HEAD_DIM, 1)
        o3 = (num / den).astype(BF16)
        after3 = (after2.astype(F32) + dot(o3, mwv[3])).astype(BF16)
        n4 = normed(after3, g4[...])
        hidden = jax.nn.gelu(dot(n4, fuv[...]), approximate=True).astype(BF16)
        encoded = (after3.astype(F32) + dot(hidden, fdv[...])).astype(BF16)
        enc[part] = encoded.reshape(tc, agents, width)
        return carry

    lax.fori_loop(0, chunks, one_chunk, 0)

    for g in range(ny):
        piece = enc[:, g * ac : (g + 1) * ac].reshape(block, width)
        out[g * ac : (g + 1) * ac] = dot(to_agents, piece).astype(BF16).reshape(ac, steps, width)

    for k in range(1, 5):
        @pl.when(exists[k])
        def _():
            p_copy(k).wait_send()
            for c in range(chunks):
                h_copy(k, c).wait_send()
    for c in range(chunks):
        for d in range(1, ny):
            b_copy(d, c).wait_send()


def local(n_region, ny, *args):
    features, neighbours, polylines = args[0:3]
    gains = [g.reshape(1, -1) for g in args[3:7]]
    tw, sw, mw, fu, fd = args[7:12]
    agents, steps, width = features.shape
    ac = agents // ny
    chunks = 4
    tc = steps // chunks
    polys = polylines.shape[0]
    anyspace = pl.BlockSpec(memory_space=pl.ANY)
    vmem = pl.BlockSpec(memory_space=pltpu.VMEM)
    dma = pltpu.SemaphoreType.DMA
    return pl.pallas_call(
        functools.partial(kernel, n_region, ny, chunks),
        out_shape=jax.ShapeDtypeStruct(features.shape, BF16),
        in_specs=[anyspace, vmem, anyspace] + [vmem] * 4 + [anyspace] * 5,
        out_specs=vmem,
        scratch_shapes=[
            pltpu.VMEM((ny, ac, steps, width), BF16),
            pltpu.VMEM((ny, ac, steps, 3 * width), BF16),
            pltpu.VMEM((ny, ac, steps, width), BF16),
            pltpu.VMEM((ny, steps, ac, width), BF16),
            pltpu.VMEM((5, steps, agents, width), BF16),
            pltpu.VMEM((5, polys, width), BF16),
            pltpu.VMEM((width, 5 * polys), BF16),
            pltpu.VMEM((HEADS, 5 * polys, width), BF16),
            pltpu.VMEM((5, tc, agents, width), BF16),
            pltpu.VMEM((5, tc, agents, width), BF16),
            pltpu.VMEM((steps, agents, width), BF16),
            pltpu.VMEM(tw.shape, BF16),
            pltpu.VMEM(sw.shape, BF16),
            pltpu.VMEM(mw.shape, BF16),
            pltpu.VMEM(fu.shape, BF16),
            pltpu.VMEM(fd.shape, BF16),
            dma((2,)),
            dma((5,)),
            dma((ny - 1,)),
            dma((ny - 1,)),
            dma((4,)),
            dma((4,)),
            dma((ny - 1, chunks)),
            dma((ny - 1, chunks)),
            dma((4, chunks)),
            dma((4, chunks)),
        ],
        compiler_params=pltpu.CompilerParams(
            collective_id=0, has_side_effects=True, vmem_limit_bytes=60 * 1024 * 1024
        ),
    )(features, neighbours, polylines, *gains, tw, sw, mw, fu, fd)


def solution(mesh):
    in_specs = (P("region", "step", None), P("region", None), P("region", None)) + (P(),) * 9
    body = functools.partial(local, mesh.shape["region"], mesh.shape["step"])
    return jax.shard_map(
        body, mesh=mesh, in_specs=in_specs, out_specs=P("region", "step", None), check_vma=False
    )
```

```python
import functools
import math

import jax
import jax.numpy as jnp
from jax import lax
from jax.experimental import pallas as pl
from jax.experimental.pallas import tpu as pltpu
from jax.sharding import PartitionSpec as P

HEADS = 8
HEAD_DIM = 32
GRID_W = 4
BF16 = jnp.bfloat16
F32 = jnp.float32
QSCALE = HEAD_DIM ** (-0.5) * math.log2(math.e)
OPPOSITE = (0, 2, 1, 4, 3)
MESH = pl.DeviceIdType.MESH


def dot(a, b):
    return jnp.dot(a, b, preferred_element_type=F32)


def dot_nt(a, b):
    return lax.dot_general(a, b, (((1,), (1,)), ((), ())), preferred_element_type=F32)


def normed(x, gain):
    xf = x.astype(F32)
    inv = lax.rsqrt(jnp.mean(xf * xf, axis=-1, keepdims=True) + 1e-06)
    return (xf * inv * gain).astype(BF16)


def small_attention(q, keys, values, head_rows, bias=None):
    rows, width = q.shape
    stacked = jnp.concatenate([q * head_rows[h : h + 1].astype(BF16) for h in range(HEADS)], axis=0)
    scores = dot_nt(stacked, keys)
    if bias is not None:
        scores = (scores.reshape(HEADS, rows, -1) + bias[None]).reshape(HEADS * rows, -1)
    top = jnp.max(scores, axis=-1, keepdims=True)
    expo = jnp.exp2(scores - top)
    total = jnp.sum(expo, axis=-1, keepdims=True)
    out = dot(expo.astype(BF16), values)
    num = out[0:rows]
    den = jnp.broadcast_to(total[0:rows], (rows, width))
    for h in range(1, HEADS):
        here = head_rows[h : h + 1] > 0.5
        num = jnp.where(here, out[h * rows : (h + 1) * rows], num)
        den = jnp.where(here, total[h * rows : (h + 1) * rows], den)
    return (num / den).astype(BF16)


def kernel(
    n_region, ny, chunks, split,
    feat, nbr, poly, g1, g2, g3, g4, tw, sw, mw, fu, fd,
    out,
    fall, after, back, cand, polys, kpt, rhs, k2, v2, enc, twv, swv, mwv, fuv, fdv,
    own_sem, w_sem, a_send, a_recv, p_send, p_recv, b_send, b_recv, h_send, h_recv, f_send,
):
    region = lax.axis_index("region")
    step = lax.axis_index("step")
    column = lax.rem(region, GRID_W)
    exists = (None, column != 0, column != GRID_W - 1, region >= GRID_W, region < n_region - GRID_W)
    others = (region, region - 1, region + 1, region - GRID_W, region + GRID_W)
    ac, steps = fall.shape[1], fall.shape[2]
    agents, width = cand.shape[2], cand.shape[3]
    tc = steps // chunks
    pieces = chunks * split
    tp = tc // split
    rows = tc * agents
    left_mid, right_mid = column == 1, column == 2
    relays = (left_mid & exists[3]) | (right_mid & exists[4])
    partner = jnp.where(left_mid, region - (GRID_W - 1), region + (GRID_W - 1))
    relay_from = jnp.where(left_mid, 2, 1)
    relay_to = jnp.where(left_mid, 4, 3)
    direct = (
        None,
        exists[1],
        exists[2],
        exists[3] & jnp.logical_not(right_mid),
        exists[4] & jnp.logical_not(left_mid),
    )
    plain = (
        None,
        exists[1] & jnp.logical_not(relays & right_mid),
        exists[2] & jnp.logical_not(relays & left_mid),
        exists[3],
        exists[4],
    )
    block = ac * steps
    groups = a_recv.shape[1]
    ga = ac // groups

    barrier = pltpu.get_barrier_semaphore()
    peers = [lax.rem(step + d, ny) for d in range(1, ny)]
    for peer in peers:
        pl.semaphore_signal(barrier, inc=1, device_id=(region, peer), device_id_type=MESH)
    for k in range(1, 5):
        @pl.when(exists[k])
        def _():
            pl.semaphore_signal(barrier, inc=1, device_id=(others[k], step), device_id_type=MESH)

    @pl.when(relays)
    def _():
        pl.semaphore_signal(barrier, inc=1, device_id=(partner, step), device_id_type=MESH)

    def own_copy():
        return pltpu.make_async_copy(
            feat.at[pl.ds(pl.multiple_of(step * ac, ac), ac)], fall.at[step], own_sem.at[0]
        )

    def poly_copy():
        return pltpu.make_async_copy(poly, polys.at[0], own_sem.at[1])

    weights = ((tw, twv), (sw, swv), (mw, mwv), (fu, fuv), (fd, fdv))

    def weight_copy(i):
        return pltpu.make_async_copy(weights[i][0], weights[i][1], w_sem.at[i])

    own_copy().start()
    poly_copy().start()
    for i in range(5):
        weight_copy(i).start()

    greeted = ny - 1 + relays.astype(jnp.int32)
    for k in range(1, 5):
        greeted = greeted + exists[k].astype(jnp.int32)
    pl.semaphore_wait(barrier, greeted)

    def a_copy(d, g):
        peer = peers[d - 1]
        return pltpu.make_async_remote_copy(
            src_ref=feat.at[pl.ds(peer * ac + g * ga, ga)],
            dst_ref=fall.at[step, pl.ds(g * ga, ga)],
            send_sem=a_send.at[d - 1, g],
            recv_sem=a_recv.at[d - 1, g],
            device_id=(region, peer),
            device_id_type=MESH,
        )

    def p_copy(k):
        return pltpu.make_async_remote_copy(
            src_ref=poly,
            dst_ref=polys.at[OPPOSITE[k]],
            send_sem=p_send.at[k - 1],
            recv_sem=p_recv.at[OPPOSITE[k] - 1],
            device_id=(others[k], step),
            device_id_type=MESH,
        )

    def piece_of(c):
        return pl.ds(c * tp, tp)

    def b_copy(d, c):
        peer = peers[d - 1]
        return pltpu.make_async_remote_copy(
            src_ref=back.at[peer, piece_of(c)],
            dst_ref=cand.at[0, piece_of(c), pl.ds(pl.multiple_of(step * ac, ac), ac)],
            send_sem=b_send.at[d - 1, c],
            recv_sem=b_recv.at[d - 1, c],
            device_id=(region, peer),
            device_id_type=MESH,
        )

    def h_copy(k, c):
        return pltpu.make_async_remote_copy(
            src_ref=cand.at[0, piece_of(c)],
            dst_ref=cand.at[OPPOSITE[k], piece_of(c)],
            send_sem=h_send.at[k - 1, c],
            recv_sem=h_recv.at[OPPOSITE[k] - 1, c],
            device_id=(others[k], step),
            device_id_type=MESH,
        )

    def h_arrival(k, c):
        return pltpu.make_async_remote_copy(
            src_ref=cand.at[0, piece_of(c)],
            dst_ref=cand.at[k, piece_of(c)],
            send_sem=f_send.at[c],
            recv_sem=h_recv.at[k - 1, c],
            device_id=(region, peers[0]),
            device_id_type=MESH,
        )

    def f_copy(c):
        return pltpu.make_async_remote_copy(
            src_ref=cand.at[relay_from, piece_of(c)],
            dst_ref=cand.at[relay_to, piece_of(c)],
            send_sem=f_send.at[c],
            recv_sem=h_recv.at[relay_to - 1, c],
            device_id=(partner, step),
            device_id_type=MESH,
        )

    def pass_on(c):
        @pl.when(relays)
        def _():
            h_arrival(relay_from, c).wait_recv()
            f_copy(c).start()

    def p_arrival(k):
        return pltpu.make_async_remote_copy(
            src_ref=poly,
            dst_ref=polys.at[k],
            send_sem=p_send.at[k - 1],
            recv_sem=p_recv.at[k - 1],
            device_id=(others[k], step),
            device_id_type=MESH,
        )

    for g in range(groups):
        for d in range(1, ny):
            a_copy(d, g).start()
    for k in range(1, 5):
        @pl.when(exists[k])
        def _():
            p_copy(k).start()

    head_rows = (
        lax.broadcasted_iota(jnp.int32, (HEADS, width), 1) // HEAD_DIM
        == lax.broadcasted_iota(jnp.int32, (HEADS, width), 0)
    ).astype(F32)
    row_i = lax.broadcasted_iota(jnp.int32, (block, block), 0)
    col_j = lax.broadcasted_iota(jnp.int32, (block, block), 1)
    to_steps = (col_j == lax.rem(row_i, ac) * steps + row_i // ac).astype(F32).astype(BF16)
    to_agents = (col_j == lax.rem(row_i, steps) * ac + row_i // steps).astype(F32).astype(BF16)

    slot = lax.broadcasted_iota(jnp.int32, (agents, 1), 0)
    ids = jnp.concatenate([other * agents + slot for other in others + (others[0],)], axis=0)
    wide = jnp.concatenate([nbr[...], nbr[...]], axis=1)
    self_id = region * agents + lax.rem(
        lax.broadcasted_iota(jnp.int32, (1, 2 * agents), 1), agents
    )
    linked = jnp.where(self_id == ids, 1.0, 0.0)
    for n in range(nbr.shape[0]):
        linked = jnp.where(wide[n : n + 1] == ids, 1.0, linked)
    bias = jnp.where(linked > 0.5, 0.0, -1e30).T[0:agents, 0 : 5 * agents]

    own_copy().wait()
    weight_copy(0).wait()

    def one_group(g, carry):
        for d in range(1, ny):
            a_copy(d, g).wait_recv()
        mine = pl.ds(g * ga, ga)
        x = fall[:, mine].reshape(ny * ga * steps, width)
        n1 = normed(x, g1[...])
        q = (dot(n1, twv[0]) * QSCALE).astype(BF16).reshape(ny, ga, steps, width)
        keys = dot(n1, twv[1]).astype(BF16).reshape(ny, ga, steps, width)
        values = dot(n1, twv[2]).astype(BF16).reshape(ny, ga, steps, width)
        every = ny * steps
        mixes = []
        for a in range(ga):
            mixed = small_attention(
                q[:, a].reshape(every, width),
                keys[:, a].reshape(every, width),
                values[:, a].reshape(every, width),
                head_rows,
            )
            mixes.append(mixed.reshape(ny, 1, steps, width))
        o1 = jnp.concatenate(mixes, axis=1).reshape(ny * ga * steps, width)
        after1 = (x.astype(F32) + dot(o1, twv[3])).astype(BF16)
        after[:, mine] = after1.reshape(ny, ga, steps, width)
        return carry

    lax.fori_loop(0, groups, one_group, 0)
    for y in range(ny):
        moved = dot(to_steps, after[y].reshape(block, width))
        back[y] = moved.astype(BF16).reshape(steps, ac, width)

    for c in range(pieces):
        for d in range(1, ny):
            b_copy(d, c).start()

    mine = pltpu.make_async_copy(
        back.at[step], cand.at[0, :, pl.ds(pl.multiple_of(step * ac, ac), ac)], own_sem.at[0]
    )
    mine.start()

    poly_copy().wait()
    weight_copy(2).wait()
    for k in range(1, 5):
        @pl.when(exists[k])
        def _():
            p_arrival(k).wait_recv()

        @pl.when(jnp.logical_not(exists[k]))
        def _():
            polys[k] = polys[0]
            cand[k] = jnp.zeros_like(cand[k])
    count = polys.shape[1]
    for k in range(5):
        here = slice(k * count, (k + 1) * count)
        kpt[:, here] = dot(polys[k], mwv[1]).T.astype(BF16)
        valid = jnp.float32(1.0) if k == 0 else jnp.where(exists[k], 1.0, 0.0)
        values = (dot(polys[k], mwv[2]) * valid).astype(BF16)
        for h in range(HEADS):
            rhs[h, here] = jnp.where(head_rows[h : h + 1] > 0.5, values, valid.astype(BF16))

    mine.wait()
    for c in range(pieces):
        for d in range(1, ny):
            b_copy(d, c).wait_recv()
        for k in (2, 1, 3, 4):
            @pl.when(direct[k])
            def _():
                h_copy(k, c).start()
    for i in (1, 3, 4):
        weight_copy(i).wait()

    for i in range(split):
        pass_on(i)

    def one_chunk(c, carry):
        for i in range(split):
            for k in range(1, 5):
                @pl.when(plain[k])
                def _():
                    h_arrival(k, c * split + i).wait_recv()

        @pl.when(c < chunks - 1)
        def _():
            for i in range(split):
                pass_on((c + 1) * split + i)

        part = pl.ds(c * tc, tc)
        for k in range(5):
            n2 = normed(cand[k, part].reshape(rows, width), g2[...])
            k2[k] = dot(n2, swv[1]).astype(BF16).reshape(tc, agents, width)
            v2[k] = dot(n2, swv[2]).astype(BF16).reshape(tc, agents, width)
            if k == 0:
                q2 = (dot(n2, swv[0]) * QSCALE).astype(BF16)
        mixes = []
        for t in range(tc):
            keys = k2[:, t].reshape(5 * agents, width)
            values = v2[:, t].reshape(5 * agents, width)
            mixes.append(
                small_attention(q2[t * agents : (t + 1) * agents], keys, values, head_rows, bias)
            )
        o2 = jnp.concatenate(mixes, axis=0)
        after2 = (cand[0, part].reshape(rows, width).astype(F32) + dot(o2, swv[3])).astype(BF16)
        n3 = normed(after2, g3[...])
        q3 = (dot(n3, mwv[0]) * QSCALE).astype(BF16)
        num = jnp.zeros((rows, width), F32)
        den = jnp.zeros((rows, width), F32)
        for h in range(HEADS):
            scores = dot(q3 * head_rows[h : h + 1].astype(BF16), kpt[...])
            top = jnp.max(scores, axis=-1, keepdims=True)
            expo = jnp.exp2(scores - top).astype(BF16)
            both = dot(expo, rhs[h])
            following = (h + 1) % HEADS
            num = jnp.where(head_rows[h : h + 1] > 0.5, both, num)
            den = jnp.where(head_rows[following : following + 1] > 0.5, both, den)
        den = pltpu.roll(den, width - HEAD_DIM, 1)
        o3 = (num / den).astype(BF16)
        after3 = (after2.astype(F32) + dot(o3, mwv[3])).astype(BF16)
        n4 = normed(after3, g4[...])
        hidden = jax.nn.gelu(dot(n4, fuv[...]), approximate=True).astype(BF16)
        encoded = (after3.astype(F32) + dot(hidden, fdv[...])).astype(BF16)
        enc[part] = encoded.reshape(tc, agents, width)
        return carry

    lax.fori_loop(0, chunks, one_chunk, 0)

    for g in range(ny):
        piece = enc[:, g * ac : (g + 1) * ac].reshape(block, width)
        out[g * ac : (g + 1) * ac] = dot(to_agents, piece).astype(BF16).reshape(ac, steps, width)

    for k in range(1, 5):
        @pl.when(exists[k])
        def _():
            p_copy(k).wait_send()

        @pl.when(direct[k])
        def _():
            for c in range(pieces):
                h_copy(k, c).wait_send()

    @pl.when(relays)
    def _():
        for c in range(pieces):
            f_copy(c).wait_send()

    for c in range(pieces):
        for d in range(1, ny):
            b_copy(d, c).wait_send()
    for g in range(groups):
        for d in range(1, ny):
            a_copy(d, g).wait_send()


def local(n_region, ny, *args):
    features, neighbours, polylines = args[0:3]
    gains = [g.reshape(1, -1) for g in args[3:7]]
    tw, sw, mw, fu, fd = args[7:12]
    agents, steps, width = features.shape
    ac = agents // ny
    chunks = 4
    tc = steps // chunks
    groups, split = 4, 2
    pieces = chunks * split
    polys = polylines.shape[0]
    anyspace = pl.BlockSpec(memory_space=pl.ANY)
    vmem = pl.BlockSpec(memory_space=pltpu.VMEM)
    dma = pltpu.SemaphoreType.DMA
    return pl.pallas_call(
        functools.partial(kernel, n_region, ny, chunks, split),
        out_shape=jax.ShapeDtypeStruct(features.shape, BF16),
        in_specs=[anyspace, vmem, anyspace] + [vmem] * 4 + [anyspace] * 5,
        out_specs=vmem,
        scratch_shapes=[
            pltpu.VMEM((ny, ac, steps, width), BF16),
            pltpu.VMEM((ny, ac, steps, width), BF16),
            pltpu.VMEM((ny, steps, ac, width), BF16),
            pltpu.VMEM((5, steps, agents, width), BF16),
            pltpu.VMEM((5, polys, width), BF16),
            pltpu.VMEM((width, 5 * polys), BF16),
            pltpu.VMEM((HEADS, 5 * polys, width), BF16),
            pltpu.VMEM((5, tc, agents, width), BF16),
            pltpu.VMEM((5, tc, agents, width), BF16),
            pltpu.VMEM((steps, agents, width), BF16),
            pltpu.VMEM(tw.shape, BF16),
            pltpu.VMEM(sw.shape, BF16),
            pltpu.VMEM(mw.shape, BF16),
            pltpu.VMEM(fu.shape, BF16),
            pltpu.VMEM(fd.shape, BF16),
            dma((2,)),
            dma((5,)),
            dma((ny - 1, groups)),
            dma((ny - 1, groups)),
            dma((4,)),
            dma((4,)),
            dma((ny - 1, pieces)),
            dma((ny - 1, pieces)),
            dma((4, pieces)),
            dma((4, pieces)),
            dma((pieces,)),
        ],
        compiler_params=pltpu.CompilerParams(
            collective_id=0, has_side_effects=True, vmem_limit_bytes=60 * 1024 * 1024
        ),
    )(features, neighbours.T, polylines, *gains, tw, sw, mw, fu, fd)


def solution(mesh):
    in_specs = (P("region", "step", None), P("region", None), P("region", None)) + (P(),) * 9
    body = functools.partial(local, mesh.shape["region"], mesh.shape["step"])
    return jax.shard_map(
        body, mesh=mesh, in_specs=in_specs, out_specs=P("region", "step", None), check_vma=False
    )
```

```python
import functools
import math

import jax
import jax.numpy as jnp
from jax import lax
from jax.experimental import pallas as pl
from jax.experimental.pallas import tpu as pltpu
from jax.sharding import PartitionSpec as P

HEADS = 8
HEAD_DIM = 32
GRID_W = 4
BF16 = jnp.bfloat16
F32 = jnp.float32
QSCALE = HEAD_DIM ** (-0.5) * math.log2(math.e)
OPPOSITE = (0, 2, 1, 4, 3)
MESH = pl.DeviceIdType.MESH


def dot(a, b):
    return jnp.dot(a, b, preferred_element_type=F32)


def dot_nt(a, b):
    return lax.dot_general(a, b, (((1,), (1,)), ((), ())), preferred_element_type=F32)


def normed(x, gain):
    xf = x.astype(F32)
    inv = lax.rsqrt(jnp.mean(xf * xf, axis=-1, keepdims=True) + 1e-06)
    return (xf * inv * gain).astype(BF16)


def small_attention(q, keys, values, head_rows, bias=None):
    rows, width = q.shape
    stacked = jnp.concatenate([q * head_rows[h : h + 1].astype(BF16) for h in range(HEADS)], axis=0)
    scores = dot_nt(stacked, keys)
    if bias is not None:
        scores = (scores.reshape(HEADS, rows, -1) + bias[None]).reshape(HEADS * rows, -1)
    top = jnp.max(scores, axis=-1, keepdims=True)
    expo = jnp.exp2(scores - top)
    total = jnp.sum(expo, axis=-1, keepdims=True)
    out = dot(expo.astype(BF16), values)
    num = out[0:rows]
    den = jnp.broadcast_to(total[0:rows], (rows, width))
    for h in range(1, HEADS):
        here = head_rows[h : h + 1] > 0.5
        num = jnp.where(here, out[h * rows : (h + 1) * rows], num)
        den = jnp.where(here, total[h * rows : (h + 1) * rows], den)
    return (num / den).astype(BF16)


def kernel(
    n_region, ny, chunks, split,
    feat, nbr_in, poly, g1_in, g2_in, g3_in, g4_in, tw, sw, mw, fu, fd,
    out,
    fall, after, back, cand, polys, kpt, rhs, k2, v2, enc, nbr, g1, g2, g3, g4, twv, swv, mwv, fuv, fdv,
    own_sem, w_sem, o_sem, a_send, a_recv, p_send, p_recv, b_send, b_recv, h_send, h_recv, f_send,
):
    region = lax.axis_index("region")
    step = lax.axis_index("step")
    column = lax.rem(region, GRID_W)
    exists = (None, column != 0, column != GRID_W - 1, region >= GRID_W, region < n_region - GRID_W)
    others = (region, region - 1, region + 1, region - GRID_W, region + GRID_W)
    ac, steps = fall.shape[1], fall.shape[2]
    agents, width = cand.shape[2], cand.shape[3]
    tc = steps // chunks
    pieces = chunks * split
    tp = tc // split
    rows = tc * agents
    left_mid, right_mid = column == 1, column == 2
    relays = (left_mid & exists[3]) | (right_mid & exists[4])
    partner = jnp.where(left_mid, region - (GRID_W - 1), region + (GRID_W - 1))
    relay_from = jnp.where(left_mid, 2, 1)
    relay_to = jnp.where(left_mid, 4, 3)
    direct = (
        None,
        exists[1],
        exists[2],
        exists[3] & jnp.logical_not(right_mid),
        exists[4] & jnp.logical_not(left_mid),
    )
    plain = (
        None,
        exists[1] & jnp.logical_not(relays & right_mid),
        exists[2] & jnp.logical_not(relays & left_mid),
        exists[3],
        exists[4],
    )
    block = ac * steps
    groups = a_recv.shape[1]
    ga = ac // groups

    barrier = pltpu.get_barrier_semaphore()
    peers = [lax.rem(step + d, ny) for d in range(1, ny)]
    for peer in peers:
        pl.semaphore_signal(barrier, inc=1, device_id=(region, peer), device_id_type=MESH)
    for k in range(1, 5):
        @pl.when(exists[k])
        def _():
            pl.semaphore_signal(barrier, inc=1, device_id=(others[k], step), device_id_type=MESH)

    @pl.when(relays)
    def _():
        pl.semaphore_signal(barrier, inc=1, device_id=(partner, step), device_id_type=MESH)

    def own_copy():
        return pltpu.make_async_copy(
            feat.at[pl.ds(pl.multiple_of(step * ac, ac), ac)], fall.at[step], own_sem.at[0]
        )

    def poly_copy():
        return pltpu.make_async_copy(poly, polys.at[0], own_sem.at[1])

    weights = (
        (tw, twv), (sw, swv), (mw, mwv), (fu, fuv), (fd, fdv),
        (nbr_in, nbr), (g1_in, g1), (g2_in, g2), (g3_in, g3), (g4_in, g4),
    )

    def weight_copy(i):
        return pltpu.make_async_copy(weights[i][0], weights[i][1], w_sem.at[i])

    own_copy().start()
    poly_copy().start()
    for i in (5, 6, 0, 2, 1, 3, 4, 7, 8, 9):
        weight_copy(i).start()

    greeted = ny - 1 + relays.astype(jnp.int32)
    for k in range(1, 5):
        greeted = greeted + exists[k].astype(jnp.int32)
    pl.semaphore_wait(barrier, greeted)

    def a_copy(d, g):
        peer = peers[d - 1]
        return pltpu.make_async_remote_copy(
            src_ref=feat.at[pl.ds(peer * ac + g * ga, ga)],
            dst_ref=fall.at[step, pl.ds(g * ga, ga)],
            send_sem=a_send.at[d - 1, g],
            recv_sem=a_recv.at[d - 1, g],
            device_id=(region, peer),
            device_id_type=MESH,
        )

    def p_copy(k):
        return pltpu.make_async_remote_copy(
            src_ref=poly,
            dst_ref=polys.at[OPPOSITE[k]],
            send_sem=p_send.at[k - 1],
            recv_sem=p_recv.at[OPPOSITE[k] - 1],
            device_id=(others[k], step),
            device_id_type=MESH,
        )

    def piece_of(c):
        return pl.ds(c * tp, tp)

    def b_copy(d, c):
        peer = peers[d - 1]
        return pltpu.make_async_remote_copy(
            src_ref=back.at[peer, piece_of(c)],
            dst_ref=cand.at[0, piece_of(c), pl.ds(pl.multiple_of(step * ac, ac), ac)],
            send_sem=b_send.at[d - 1, c],
            recv_sem=b_recv.at[d - 1, c],
            device_id=(region, peer),
            device_id_type=MESH,
        )

    def h_copy(k, c):
        return pltpu.make_async_remote_copy(
            src_ref=cand.at[0, piece_of(c)],
            dst_ref=cand.at[OPPOSITE[k], piece_of(c)],
            send_sem=h_send.at[k - 1, c],
            recv_sem=h_recv.at[OPPOSITE[k] - 1, c],
            device_id=(others[k], step),
            device_id_type=MESH,
        )

    def h_arrival(k, c):
        return pltpu.make_async_remote_copy(
            src_ref=cand.at[0, piece_of(c)],
            dst_ref=cand.at[k, piece_of(c)],
            send_sem=f_send.at[c],
            recv_sem=h_recv.at[k - 1, c],
            device_id=(region, peers[0]),
            device_id_type=MESH,
        )

    def f_copy(c):
        return pltpu.make_async_remote_copy(
            src_ref=cand.at[relay_from, piece_of(c)],
            dst_ref=cand.at[relay_to, piece_of(c)],
            send_sem=f_send.at[c],
            recv_sem=h_recv.at[relay_to - 1, c],
            device_id=(partner, step),
            device_id_type=MESH,
        )

    def pass_on(c):
        @pl.when(relays)
        def _():
            h_arrival(relay_from, c).wait_recv()
            f_copy(c).start()

    def p_arrival(k):
        return pltpu.make_async_remote_copy(
            src_ref=poly,
            dst_ref=polys.at[k],
            send_sem=p_send.at[k - 1],
            recv_sem=p_recv.at[k - 1],
            device_id=(others[k], step),
            device_id_type=MESH,
        )

    for g in range(groups):
        for d in range(1, ny):
            a_copy(d, g).start()
    for k in range(1, 5):
        @pl.when(exists[k])
        def _():
            p_copy(k).start()

    head_rows = (
        lax.broadcasted_iota(jnp.int32, (HEADS, width), 1) // HEAD_DIM
        == lax.broadcasted_iota(jnp.int32, (HEADS, width), 0)
    ).astype(F32)
    row_i = lax.broadcasted_iota(jnp.int32, (block, block), 0)
    col_j = lax.broadcasted_iota(jnp.int32, (block, block), 1)
    to_steps = (col_j == lax.rem(row_i, ac) * steps + row_i // ac).astype(F32).astype(BF16)

    weight_copy(5).wait()
    slot = lax.broadcasted_iota(jnp.int32, (agents, 1), 0)
    ids = jnp.concatenate([other * agents + slot for other in others + (others[0],)], axis=0)
    wide = jnp.concatenate([nbr[...], nbr[...]], axis=1)
    self_id = region * agents + lax.rem(
        lax.broadcasted_iota(jnp.int32, (1, 2 * agents), 1), agents
    )
    linked = jnp.where(self_id == ids, 1.0, 0.0)
    for n in range(nbr.shape[0]):
        linked = jnp.where(wide[n : n + 1] == ids, 1.0, linked)
    bias = jnp.where(linked > 0.5, 0.0, -1e30).T[0:agents, 0 : 5 * agents]

    own_copy().wait()
    weight_copy(0).wait()
    weight_copy(6).wait()

    def one_group(g, carry):
        for d in range(1, ny):
            a_copy(d, g).wait_recv()
        mine = pl.ds(g * ga, ga)
        x = fall[:, mine].reshape(ny * ga * steps, width)
        n1 = normed(x, g1[...])
        q = (dot(n1, twv[0]) * QSCALE).astype(BF16).reshape(ny, ga, steps, width)
        keys = dot(n1, twv[1]).astype(BF16).reshape(ny, ga, steps, width)
        values = dot(n1, twv[2]).astype(BF16).reshape(ny, ga, steps, width)
        every = ny * steps
        mixes = []
        for a in range(ga):
            mixed = small_attention(
                q[:, a].reshape(every, width),
                keys[:, a].reshape(every, width),
                values[:, a].reshape(every, width),
                head_rows,
            )
            mixes.append(mixed.reshape(ny, 1, steps, width))
        o1 = jnp.concatenate(mixes, axis=1).reshape(ny * ga * steps, width)
        after1 = (x.astype(F32) + dot(o1, twv[3])).astype(BF16)
        after[:, mine] = after1.reshape(ny, ga, steps, width)
        return carry

    lax.fori_loop(0, groups, one_group, 0)
    for y in range(ny):
        moved = dot(to_steps, after[y].reshape(block, width))
        back[y] = moved.astype(BF16).reshape(steps, ac, width)

    for c in range(pieces):
        for d in range(1, ny):
            b_copy(d, c).start()

    mine = pltpu.make_async_copy(
        back.at[step], cand.at[0, :, pl.ds(pl.multiple_of(step * ac, ac), ac)], own_sem.at[0]
    )
    mine.start()

    poly_copy().wait()
    weight_copy(2).wait()
    for k in range(1, 5):
        @pl.when(exists[k])
        def _():
            p_arrival(k).wait_recv()

        @pl.when(jnp.logical_not(exists[k]))
        def _():
            polys[k] = polys[0]
            cand[k] = jnp.zeros_like(cand[k])
    count = polys.shape[1]
    for k in range(5):
        here = slice(k * count, (k + 1) * count)
        kpt[:, here] = dot(polys[k], mwv[1]).T.astype(BF16)
        valid = jnp.float32(1.0) if k == 0 else jnp.where(exists[k], 1.0, 0.0)
        values = (dot(polys[k], mwv[2]) * valid).astype(BF16)
        for h in range(HEADS):
            rhs[h, here] = jnp.where(head_rows[h : h + 1] > 0.5, values, valid.astype(BF16))

    mine.wait()
    def send_own(c):
        for i in range(split):
            for d in range(1, ny):
                b_copy(d, c * split + i).wait_recv()
            for k in (2, 1, 3, 4):
                @pl.when(direct[k])
                def _():
                    h_copy(k, c * split + i).start()

    def result_copy(c):
        return pltpu.make_async_copy(enc.at[pl.ds(c * tc, tc)], out.at[pl.ds(c * tc, tc)], o_sem.at[c])

    send_own(0)
    for i in (1, 3, 4, 7, 8, 9):
        weight_copy(i).wait()

    for i in range(split):
        pass_on(i)
    send_own(1)

    def one_chunk(c, carry):
        for i in range(split):
            for k in range(1, 5):
                @pl.when(plain[k])
                def _():
                    h_arrival(k, c * split + i).wait_recv()

        @pl.when(c < chunks - 2)
        def _():
            send_own(c + 2)

        part = pl.ds(c * tc, tc)
        for k in range(5):
            n2 = normed(cand[k, part].reshape(rows, width), g2[...])
            k2[k] = dot(n2, swv[1]).astype(BF16).reshape(tc, agents, width)
            v2[k] = dot(n2, swv[2]).astype(BF16).reshape(tc, agents, width)
            if k == 0:
                q2 = (dot(n2, swv[0]) * QSCALE).astype(BF16)
        mixes = []
        for t in range(tc):
            keys = k2[:, t].reshape(5 * agents, width)
            values = v2[:, t].reshape(5 * agents, width)
            mixes.append(
                small_attention(q2[t * agents : (t + 1) * agents], keys, values, head_rows, bias)
            )
        o2 = jnp.concatenate(mixes, axis=0)

        @pl.when(c < chunks - 1)
        def _():
            for i in range(split):
                pass_on((c + 1) * split + i)

        after2 = (cand[0, part].reshape(rows, width).astype(F32) + dot(o2, swv[3])).astype(BF16)
        n3 = normed(after2, g3[...])
        q3 = (dot(n3, mwv[0]) * QSCALE).astype(BF16)
        num = jnp.zeros((rows, width), F32)
        den = jnp.zeros((rows, width), F32)
        for h in range(HEADS):
            scores = dot(q3 * head_rows[h : h + 1].astype(BF16), kpt[...])
            top = jnp.max(scores, axis=-1, keepdims=True)
            expo = jnp.exp2(scores - top).astype(BF16)
            both = dot(expo, rhs[h])
            following = (h + 1) % HEADS
            num = jnp.where(head_rows[h : h + 1] > 0.5, both, num)
            den = jnp.where(head_rows[following : following + 1] > 0.5, both, den)
        den = pltpu.roll(den, width - HEAD_DIM, 1)
        o3 = (num / den).astype(BF16)
        after3 = (after2.astype(F32) + dot(o3, mwv[3])).astype(BF16)
        n4 = normed(after3, g4[...])
        hidden = jax.nn.gelu(dot(n4, fuv[...]), approximate=True).astype(BF16)
        encoded = (after3.astype(F32) + dot(hidden, fdv[...])).astype(BF16)
        enc[part] = encoded.reshape(tc, agents, width)
        result_copy(c).start()
        return carry

    lax.fori_loop(0, chunks, one_chunk, 0)

    for c in range(chunks):
        result_copy(c).wait()
    for k in range(1, 5):
        @pl.when(exists[k])
        def _():
            p_copy(k).wait_send()

        @pl.when(direct[k])
        def _():
            for c in range(pieces):
                h_copy(k, c).wait_send()

    @pl.when(relays)
    def _():
        for c in range(pieces):
            f_copy(c).wait_send()

    for c in range(pieces):
        for d in range(1, ny):
            b_copy(d, c).wait_send()
    for g in range(groups):
        for d in range(1, ny):
            a_copy(d, g).wait_send()


def agents_first(x, out):
    steps, agents, width = x.shape
    ac = steps
    block = steps * ac
    row_i = lax.broadcasted_iota(jnp.int32, (block, block), 0)
    col_j = lax.broadcasted_iota(jnp.int32, (block, block), 1)
    to_agents = (col_j == lax.rem(row_i, steps) * ac + row_i // steps).astype(F32).astype(BF16)
    for g in range(agents // ac):
        mine = slice(g * ac, (g + 1) * ac)
        moved = dot(to_agents, x[:, mine].reshape(block, width))
        out[mine] = moved.astype(BF16).reshape(ac, steps, width)


def local(n_region, ny, *args):
    features, neighbours, polylines = args[0:3]
    gains = [g.reshape(1, -1) for g in args[3:7]]
    tw, sw, mw, fu, fd = args[7:12]
    agents, steps, width = features.shape
    ac = agents // ny
    chunks = 4
    tc = steps // chunks
    groups, split = 4, 2
    pieces = chunks * split
    polys = polylines.shape[0]
    anyspace = pl.BlockSpec(memory_space=pl.ANY)
    dma = pltpu.SemaphoreType.DMA
    encoded = pl.pallas_call(
        functools.partial(kernel, n_region, ny, chunks, split),
        out_shape=jax.ShapeDtypeStruct((steps, agents, width), BF16),
        in_specs=[anyspace] * 12,
        out_specs=anyspace,
        scratch_shapes=[
            pltpu.VMEM((ny, ac, steps, width), BF16),
            pltpu.VMEM((ny, ac, steps, width), BF16),
            pltpu.VMEM((ny, steps, ac, width), BF16),
            pltpu.VMEM((5, steps, agents, width), BF16),
            pltpu.VMEM((5, polys, width), BF16),
            pltpu.VMEM((width, 5 * polys), BF16),
            pltpu.VMEM((HEADS, 5 * polys, width), BF16),
            pltpu.VMEM((5, tc, agents, width), BF16),
            pltpu.VMEM((5, tc, agents, width), BF16),
            pltpu.VMEM((steps, agents, width), BF16),
            pltpu.VMEM((neighbours.shape[1], agents), jnp.int32),
            pltpu.VMEM((1, width), F32),
            pltpu.VMEM((1, width), F32),
            pltpu.VMEM((1, width), F32),
            pltpu.VMEM((1, width), F32),
            pltpu.VMEM(tw.shape, BF16),
            pltpu.VMEM(sw.shape, BF16),
            pltpu.VMEM(mw.shape, BF16),
            pltpu.VMEM(fu.shape, BF16),
            pltpu.VMEM(fd.shape, BF16),
            dma((2,)),
            dma((10,)),
            dma((chunks,)),
            dma((ny - 1, groups)),
            dma((ny - 1, groups)),
            dma((4,)),
            dma((4,)),
            dma((ny - 1, pieces)),
            dma((ny - 1, pieces)),
            dma((4, pieces)),
            dma((4, pieces)),
            dma((pieces,)),
        ],
        compiler_params=pltpu.CompilerParams(
            collective_id=0, has_side_effects=True, vmem_limit_bytes=60 * 1024 * 1024
        ),
    )(features, neighbours.T, polylines, *gains, tw, sw, mw, fu, fd)
    return pl.pallas_call(
        agents_first,
        out_shape=jax.ShapeDtypeStruct(features.shape, BF16),
        in_specs=[pl.BlockSpec(memory_space=pltpu.VMEM)],
        out_specs=pl.BlockSpec(memory_space=pltpu.VMEM),
    )(encoded)


def solution(mesh):
    in_specs = (P("region", "step", None), P("region", None), P("region", None)) + (P(),) * 9
    body = functools.partial(local, mesh.shape["region"], mesh.shape["step"])
    return jax.shard_map(
        body, mesh=mesh, in_specs=in_specs, out_specs=P("region", "step", None), check_vma=False
    )
```

```python
import functools
import math

import jax
import jax.numpy as jnp
from jax import lax
from jax.experimental import pallas as pl
from jax.experimental.pallas import tpu as pltpu
from jax.sharding import PartitionSpec as P

HEADS = 8
HEAD_DIM = 32
GRID_W = 4
BF16 = jnp.bfloat16
F32 = jnp.float32
QSCALE = HEAD_DIM ** (-0.5) * math.log2(math.e)
OPPOSITE = (0, 2, 1, 4, 3)
MESH = pl.DeviceIdType.MESH


def dot(a, b):
    return jnp.dot(a, b, preferred_element_type=F32)


def dot_nt(a, b):
    return lax.dot_general(a, b, (((1,), (1,)), ((), ())), preferred_element_type=F32)


def normed(x, gain):
    xf = x.astype(F32)
    inv = lax.rsqrt(jnp.mean(xf * xf, axis=-1, keepdims=True) + 1e-06)
    return (xf * inv * gain).astype(BF16)


def partial_attention(q, keys, values, head_rows, bias=None):
    rows, width = q.shape
    stacked = jnp.concatenate([q * head_rows[h : h + 1].astype(BF16) for h in range(HEADS)], axis=0)
    scores = dot_nt(stacked, keys)
    if bias is not None:
        scores = (scores.reshape(HEADS, rows, -1) + bias[None]).reshape(HEADS * rows, -1)
    top = jnp.max(scores, axis=-1, keepdims=True)
    expo = jnp.exp2(scores - top)
    total = jnp.sum(expo, axis=-1, keepdims=True)
    out = dot(expo.astype(BF16), values)
    picked = [out[0:rows]] + [jnp.broadcast_to(x[0:rows], (rows, width)) for x in (total, top)]
    for h in range(1, HEADS):
        here = head_rows[h : h + 1] > 0.5
        mine = slice(h * rows, (h + 1) * rows)
        picked = [jnp.where(here, x[mine], p) for x, p in zip((out, total, top), picked)]
    return picked


def small_attention(q, keys, values, head_rows):
    num, den, _ = partial_attention(q, keys, values, head_rows)
    return (num / den).astype(BF16)


def kernel(
    n_region, ny, chunks, split,
    feat, nbr_in, poly, g1_in, g2_in, g3_in, g4_in, tw, sw, mw, fu, fd,
    out,
    fall, after, back, cand, polys, kp, vext, k2, v2, q2, own, enc, nbr, g1, g2, g3, g4, twv, swv, mwv, fuv, fdv,
    own_sem, w_sem, o_sem, a_send, a_recv, p_send, p_recv, b_send, b_recv, h_send, h_recv,
):
    region = lax.axis_index("region")
    step = lax.axis_index("step")
    column = lax.rem(region, GRID_W)
    exists = (None, column != 0, column != GRID_W - 1, region >= GRID_W, region < n_region - GRID_W)
    others = (region, region - 1, region + 1, region - GRID_W, region + GRID_W)
    ac, steps = fall.shape[1], fall.shape[2]
    agents, width = cand.shape[2], cand.shape[3]
    tc = steps // chunks
    pieces = chunks * split
    tp = tc // split
    rows = tc * agents
    block = ac * steps
    groups = a_recv.shape[1]
    ga = ac // groups

    barrier = pltpu.get_barrier_semaphore()
    peers = [lax.rem(step + d, ny) for d in range(1, ny)]
    for peer in peers:
        pl.semaphore_signal(barrier, inc=1, device_id=(region, peer), device_id_type=MESH)
    for k in range(1, 5):
        @pl.when(exists[k])
        def _():
            pl.semaphore_signal(barrier, inc=1, device_id=(others[k], step), device_id_type=MESH)

    def own_copy():
        return pltpu.make_async_copy(
            feat.at[pl.ds(pl.multiple_of(step * ac, ac), ac)], fall.at[step], own_sem.at[0]
        )

    def poly_copy():
        return pltpu.make_async_copy(poly, polys.at[0], own_sem.at[1])

    weights = (
        (tw, twv), (sw, swv), (mw, mwv), (fu, fuv), (fd, fdv),
        (nbr_in, nbr), (g1_in, g1), (g2_in, g2), (g3_in, g3), (g4_in, g4),
    )

    def weight_copy(i):
        return pltpu.make_async_copy(weights[i][0], weights[i][1], w_sem.at[i])

    own_copy().start()
    poly_copy().start()
    for i in (5, 6, 0, 2, 1, 3, 4, 7, 8, 9):
        weight_copy(i).start()

    greeted = ny - 1
    for k in range(1, 5):
        greeted = greeted + exists[k].astype(jnp.int32)
    pl.semaphore_wait(barrier, greeted)

    def a_copy(d, g):
        peer = peers[d - 1]
        return pltpu.make_async_remote_copy(
            src_ref=feat.at[pl.ds(peer * ac + g * ga, ga)],
            dst_ref=fall.at[step, pl.ds(g * ga, ga)],
            send_sem=a_send.at[d - 1, g],
            recv_sem=a_recv.at[d - 1, g],
            device_id=(region, peer),
            device_id_type=MESH,
        )

    def p_copy(k):
        return pltpu.make_async_remote_copy(
            src_ref=poly,
            dst_ref=polys.at[OPPOSITE[k]],
            send_sem=p_send.at[k - 1],
            recv_sem=p_recv.at[OPPOSITE[k] - 1],
            device_id=(others[k], step),
            device_id_type=MESH,
        )

    def piece_of(c):
        return pl.ds(c * tp, tp)

    def b_copy(d, c):
        peer = peers[d - 1]
        return pltpu.make_async_remote_copy(
            src_ref=back.at[peer, piece_of(c)],
            dst_ref=cand.at[0, piece_of(c), pl.ds(pl.multiple_of(step * ac, ac), ac)],
            send_sem=b_send.at[d - 1, c],
            recv_sem=b_recv.at[d - 1, c],
            device_id=(region, peer),
            device_id_type=MESH,
        )

    def h_copy(k, c):
        return pltpu.make_async_remote_copy(
            src_ref=cand.at[0, piece_of(c)],
            dst_ref=cand.at[OPPOSITE[k], piece_of(c)],
            send_sem=h_send.at[k - 1, c],
            recv_sem=h_recv.at[OPPOSITE[k] - 1, c],
            device_id=(others[k], step),
            device_id_type=MESH,
        )

    def h_arrival(k, c):
        return pltpu.make_async_remote_copy(
            src_ref=cand.at[0, piece_of(c)],
            dst_ref=cand.at[k, piece_of(c)],
            send_sem=h_send.at[k - 1, c],
            recv_sem=h_recv.at[k - 1, c],
            device_id=(others[k], step),
            device_id_type=MESH,
        )

    def p_arrival(k):
        return pltpu.make_async_remote_copy(
            src_ref=poly,
            dst_ref=polys.at[k],
            send_sem=p_send.at[k - 1],
            recv_sem=p_recv.at[k - 1],
            device_id=(others[k], step),
            device_id_type=MESH,
        )

    for g in range(groups):
        for d in range(1, ny):
            a_copy(d, g).start()
    for k in range(1, 5):
        @pl.when(exists[k])
        def _():
            p_copy(k).start()

    head_rows = (
        lax.broadcasted_iota(jnp.int32, (HEADS, width), 1) // HEAD_DIM
        == lax.broadcasted_iota(jnp.int32, (HEADS, width), 0)
    ).astype(F32)
    row_i = lax.broadcasted_iota(jnp.int32, (block, block), 0)
    col_j = lax.broadcasted_iota(jnp.int32, (block, block), 1)
    to_steps = (col_j == lax.rem(row_i, ac) * steps + row_i // ac).astype(F32).astype(BF16)

    weight_copy(5).wait()
    slot = lax.broadcasted_iota(jnp.int32, (agents, 1), 0)
    ids = jnp.concatenate([other * agents + slot for other in others + (others[0],)], axis=0)
    wide = jnp.concatenate([nbr[...], nbr[...]], axis=1)
    self_id = region * agents + lax.rem(
        lax.broadcasted_iota(jnp.int32, (1, 2 * agents), 1), agents
    )
    linked = jnp.where(self_id == ids, 1.0, 0.0)
    for n in range(nbr.shape[0]):
        linked = jnp.where(wide[n : n + 1] == ids, 1.0, linked)
    bias = jnp.where(linked > 0.5, 0.0, -1e30).T[0:agents, 0 : 5 * agents]

    own_copy().wait()
    weight_copy(0).wait()
    weight_copy(6).wait()

    def one_group(g, carry):
        for d in range(1, ny):
            a_copy(d, g).wait_recv()
        mine = pl.ds(g * ga, ga)
        x = fall[:, mine].reshape(ny * ga * steps, width)
        n1 = normed(x, g1[...])
        q = (dot(n1, twv[0]) * QSCALE).astype(BF16).reshape(ny, ga, steps, width)
        keys = dot(n1, twv[1]).astype(BF16).reshape(ny, ga, steps, width)
        values = dot(n1, twv[2]).astype(BF16).reshape(ny, ga, steps, width)
        every = ny * steps
        mixes = []
        for a in range(ga):
            mixed = small_attention(
                q[:, a].reshape(every, width),
                keys[:, a].reshape(every, width),
                values[:, a].reshape(every, width),
                head_rows,
            )
            mixes.append(mixed.reshape(ny, 1, steps, width))
        o1 = jnp.concatenate(mixes, axis=1).reshape(ny * ga * steps, width)
        after1 = (x.astype(F32) + dot(o1, twv[3])).astype(BF16)
        after[:, mine] = after1.reshape(ny, ga, steps, width)
        return carry

    lax.fori_loop(0, groups, one_group, 0)
    for y in range(ny):
        moved = dot(to_steps, after[y].reshape(block, width))
        back[y] = moved.astype(BF16).reshape(steps, ac, width)

    for c in range(pieces):
        for d in range(1, ny):
            b_copy(d, c).start()

    mine = pltpu.make_async_copy(
        back.at[step], cand.at[0, :, pl.ds(pl.multiple_of(step * ac, ac), ac)], own_sem.at[0]
    )
    mine.start()

    poly_copy().wait()
    weight_copy(2).wait()
    for k in range(1, 5):
        @pl.when(exists[k])
        def _():
            p_arrival(k).wait_recv()

        @pl.when(jnp.logical_not(exists[k]))
        def _():
            polys[k] = polys[0]
            cand[k] = jnp.zeros_like(cand[k])
    count = polys.shape[1]
    for k in range(5):
        here = slice(k * count, (k + 1) * count)
        kp[here] = dot(polys[k], mwv[1]).astype(BF16)
        valid = jnp.float32(1.0) if k == 0 else jnp.where(exists[k], 1.0, 0.0)
        values = (dot(polys[k], mwv[2]) * valid).T.astype(BF16)
        ones = jnp.full((16, count), valid, F32).astype(BF16)
        for h in range(HEADS):
            vext[h, 0:HEAD_DIM, here] = values[h * HEAD_DIM : (h + 1) * HEAD_DIM]
            vext[h, HEAD_DIM : HEAD_DIM + 16, here] = ones

    mine.wait()
    def send_own(c):
        for i in range(split):
            for k in (2, 1, 3, 4):
                @pl.when(exists[k])
                def _():
                    h_copy(k, c * split + i).start()

    def result_copy(c):
        return pltpu.make_async_copy(enc.at[pl.ds(c * tc, tc)], out.at[pl.ds(c * tc, tc)], o_sem.at[c])

    for i in (1, 3, 4, 7, 8, 9):
        weight_copy(i).wait()


    late = ((column == 0) | (column == GRID_W - 1)).astype(jnp.int32)

    def own_part(c, carry):
        for i in range(split):
            for d in range(1, ny):
                b_copy(d, c * split + i).wait_recv()

        @pl.when(c < 2 - late)
        def _():
            send_own(c)

        n2 = normed(cand[0, pl.ds(c * tc, tc)].reshape(rows, width), g2[...])
        keys = dot(n2, swv[1]).astype(BF16)
        values = dot(n2, swv[2]).astype(BF16)
        queries = (dot(n2, swv[0]) * QSCALE).astype(BF16)
        q2[pl.ds(c * tc, tc)] = queries.reshape(tc, agents, width)
        for t in range(tc):
            at = slice(t * agents, (t + 1) * agents)
            found = partial_attention(
                queries[at], keys[at], values[at], head_rows, bias[:, 0:agents]
            )
            for i in range(3):
                own[i, c * tc + t] = found[i]
        return carry

    lax.fori_loop(0, chunks, own_part, 0)

    def one_chunk(c, carry):
        @pl.when((c < chunks - 1) & (late == 1))
        def _():
            send_own(c + 1)

        part = pl.ds(c * tc, tc)
        mixes = []
        for i in range(split):
            for k in range(1, 5):
                @pl.when(exists[k])
                def _():
                    h_arrival(k, c * split + i).wait_recv()

            x = cand[1:5, pl.ds(c * tc + i * tp, tp)].reshape(4 * tp * agents, width)
            n2 = normed(x, g2[...])
            k2[...] = dot(n2, swv[1]).astype(BF16).reshape(4, tp, agents, width)
            v2[...] = dot(n2, swv[2]).astype(BF16).reshape(4, tp, agents, width)
            for t in range(tp):
                at = c * tc + i * tp + t
                num, den, top = partial_attention(
                    q2[at],
                    k2[:, t].reshape(4 * agents, width),
                    v2[:, t].reshape(4 * agents, width),
                    head_rows,
                    bias[:, agents:],
                )
                high = jnp.maximum(top, own[2, at])
                theirs, ours = jnp.exp2(top - high), jnp.exp2(own[2, at] - high)
                num = num * theirs + own[0, at] * ours
                den = den * theirs + own[1, at] * ours
                mixes.append((num / den).astype(BF16))
        o2 = jnp.concatenate(mixes, axis=0)

        @pl.when((c < chunks - 2) & (late == 0))
        def _():
            send_own(c + 2)

        after2 = (cand[0, part].reshape(rows, width).astype(F32) + dot(o2, swv[3])).astype(BF16)
        n3 = normed(after2, g3[...])
        q3 = (dot(n3, mwv[0]) * QSCALE).T.astype(BF16)

        def alone(h):
            own = q3[h * HEAD_DIM : (h + 1) * HEAD_DIM]
            above = [jnp.zeros((h * HEAD_DIM, rows), BF16)] if h > 0 else []
            below = [jnp.zeros((width - (h + 1) * HEAD_DIM, rows), BF16)] if h < HEADS - 1 else []
            return jnp.concatenate(above + [own] + below, axis=0)

        def pair(j):
            return jnp.concatenate([alone(2 * j), alone(2 * j + 1)], axis=1)

        cuts = [slice(i * kp.shape[0] // 1, (i + 1) * kp.shape[0] // 1) for i in range(1)]
        parts = []
        ahead = [dot(kp[cut], pair(0)) for cut in cuts]
        for j in range(HEADS // 2):
            now = ahead
            top = functools.reduce(jnp.maximum, [jnp.max(x, axis=0, keepdims=True) for x in now])
            ahead = []
            sums = [None, None]
            for i, cut in enumerate(cuts):
                if j + 1 < HEADS // 2:
                    ahead.append(dot(kp[cut], pair(j + 1)))
                expo = jnp.exp2(now[i] - top).astype(BF16)
                for e in range(2):
                    term = dot(vext[2 * j + e, :, cut], expo[:, e * rows : (e + 1) * rows])
                    sums[e] = term if sums[e] is None else sums[e] + term
            for both in sums:
                parts.append(both[0:HEAD_DIM] / both[HEAD_DIM : HEAD_DIM + 1])
        o3 = jnp.concatenate(parts, axis=0).T.astype(BF16)
        after3 = (after2.astype(F32) + dot(o3, mwv[3])).astype(BF16)
        n4 = normed(after3, g4[...])
        hidden = jax.nn.gelu(dot(n4, fuv[...]), approximate=True).astype(BF16)
        encoded = (after3.astype(F32) + dot(hidden, fdv[...])).astype(BF16)
        enc[part] = encoded.reshape(tc, agents, width)
        result_copy(c).start()
        return carry

    lax.fori_loop(0, chunks, one_chunk, 0)

    for c in range(chunks):
        result_copy(c).wait()
    for k in range(1, 5):
        @pl.when(exists[k])
        def _():
            p_copy(k).wait_send()
            for c in range(pieces):
                h_copy(k, c).wait_send()

    for c in range(pieces):
        for d in range(1, ny):
            b_copy(d, c).wait_send()
    for g in range(groups):
        for d in range(1, ny):
            a_copy(d, g).wait_send()


def agents_first(x, out):
    steps, agents, width = x.shape
    ac = steps
    block = steps * ac
    row_i = lax.broadcasted_iota(jnp.int32, (block, block), 0)
    col_j = lax.broadcasted_iota(jnp.int32, (block, block), 1)
    to_agents = (col_j == lax.rem(row_i, steps) * ac + row_i // steps).astype(F32).astype(BF16)
    for g in range(agents // ac):
        mine = slice(g * ac, (g + 1) * ac)
        moved = dot(to_agents, x[:, mine].reshape(block, width))
        out[mine] = moved.astype(BF16).reshape(ac, steps, width)


def local(n_region, ny, *args):
    features, neighbours, polylines = args[0:3]
    gains = [g.reshape(1, -1) for g in args[3:7]]
    tw, sw, mw, fu, fd = args[7:12]
    agents, steps, width = features.shape
    ac = agents // ny
    chunks = 4
    tc = steps // chunks
    groups, split = 4, 2
    pieces = chunks * split
    polys = polylines.shape[0]
    anyspace = pl.BlockSpec(memory_space=pl.ANY)
    dma = pltpu.SemaphoreType.DMA
    encoded = pl.pallas_call(
        functools.partial(kernel, n_region, ny, chunks, split),
        out_shape=jax.ShapeDtypeStruct((steps, agents, width), BF16),
        in_specs=[anyspace] * 12,
        out_specs=anyspace,
        scratch_shapes=[
            pltpu.VMEM((ny, ac, steps, width), BF16),
            pltpu.VMEM((ny, ac, steps, width), BF16),
            pltpu.VMEM((ny, steps, ac, width), BF16),
            pltpu.VMEM((5, steps, agents, width), BF16),
            pltpu.VMEM((5, polys, width), BF16),
            pltpu.VMEM((5 * polys, width), BF16),
            pltpu.VMEM((HEADS, HEAD_DIM + 16, 5 * polys), BF16),
            pltpu.VMEM((4, tc // split, agents, width), BF16),
            pltpu.VMEM((4, tc // split, agents, width), BF16),
            pltpu.VMEM((steps, agents, width), BF16),
            pltpu.VMEM((3, steps, agents, width), F32),
            pltpu.VMEM((steps, agents, width), BF16),
            pltpu.VMEM((neighbours.shape[1], agents), jnp.int32),
            pltpu.VMEM((1, width), F32),
            pltpu.VMEM((1, width), F32),
            pltpu.VMEM((1, width), F32),
            pltpu.VMEM((1, width), F32),
            pltpu.VMEM(tw.shape, BF16),
            pltpu.VMEM(sw.shape, BF16),
            pltpu.VMEM(mw.shape, BF16),
            pltpu.VMEM(fu.shape, BF16),
            pltpu.VMEM(fd.shape, BF16),
            dma((2,)),
            dma((10,)),
            dma((chunks,)),
            dma((ny - 1, groups)),
            dma((ny - 1, groups)),
            dma((4,)),
            dma((4,)),
            dma((ny - 1, pieces)),
            dma((ny - 1, pieces)),
            dma((4, pieces)),
            dma((4, pieces)),
        ],
        compiler_params=pltpu.CompilerParams(
            collective_id=0, has_side_effects=True, vmem_limit_bytes=60 * 1024 * 1024
        ),
    )(features, neighbours.T, polylines, *gains, tw, sw, mw, fu, fd)
    return pl.pallas_call(
        agents_first,
        out_shape=jax.ShapeDtypeStruct(features.shape, BF16),
        in_specs=[pl.BlockSpec(memory_space=pltpu.VMEM)],
        out_specs=pl.BlockSpec(memory_space=pltpu.VMEM),
    )(encoded)


def solution(mesh):
    in_specs = (P("region", "step", None), P("region", None), P("region", None)) + (P(),) * 9
    body = functools.partial(local, mesh.shape["region"], mesh.shape["step"])
    return jax.shard_map(
        body, mesh=mesh, in_specs=in_specs, out_specs=P("region", "step", None), check_vma=False
    )
```

```python
import functools
import math

import jax
import jax.numpy as jnp
from jax import lax
from jax.experimental import pallas as pl
from jax.experimental.pallas import tpu as pltpu
from jax.sharding import PartitionSpec as P

HEADS = 8
HEAD_DIM = 32
GRID_W = 4
BF16 = jnp.bfloat16
F32 = jnp.float32
QSCALE = HEAD_DIM ** (-0.5) * math.log2(math.e)
OPPOSITE = (0, 2, 1, 4, 3)
MESH = pl.DeviceIdType.MESH


def dot(a, b):
    return jnp.dot(a, b, preferred_element_type=F32)


def dot_nt(a, b):
    return lax.dot_general(a, b, (((1,), (1,)), ((), ())), preferred_element_type=F32)


def normed(x, gain):
    xf = x.astype(F32)
    inv = lax.rsqrt(jnp.mean(xf * xf, axis=-1, keepdims=True) + 1e-06)
    return (xf * inv * gain).astype(BF16)


def partial_attention(q, keys, values, head_rows, bias=None):
    rows, width = q.shape
    stacked = jnp.concatenate([q * head_rows[h : h + 1].astype(BF16) for h in range(HEADS)], axis=0)
    scores = dot_nt(stacked, keys)
    if bias is not None:
        scores = (scores.reshape(HEADS, rows, -1) + bias[None]).reshape(HEADS * rows, -1)
    top = jnp.max(scores, axis=-1, keepdims=True)
    expo = jnp.exp2(scores - top)
    total = jnp.sum(expo, axis=-1, keepdims=True)
    out = dot(expo.astype(BF16), values)
    picked = [out[0:rows]] + [jnp.broadcast_to(x[0:rows], (rows, width)) for x in (total, top)]
    for h in range(1, HEADS):
        here = head_rows[h : h + 1] > 0.5
        mine = slice(h * rows, (h + 1) * rows)
        picked = [jnp.where(here, x[mine], p) for x, p in zip((out, total, top), picked)]
    return picked


def small_attention(q, keys, values, head_rows):
    num, den, _ = partial_attention(q, keys, values, head_rows)
    return (num / den).astype(BF16)


def kernel(
    n_region, ny, chunks, split,
    feat, nbr_in, poly, g1_in, g2_in, g3_in, g4_in, tw, sw, mw, fu, fd,
    out,
    fall, after, back, cand, polys, kp, vext, k2, v2, q2, own, enc, nbr, g1, g2, g3, g4, twv, swv, mwv, fuv, fdv,
    own_sem, w_sem, o_sem, a_send, a_recv, p_send, p_recv, b_send, b_recv, h_send, h_recv,
):
    region = lax.axis_index("region")
    step = lax.axis_index("step")
    column = lax.rem(region, GRID_W)
    exists = (None, column != 0, column != GRID_W - 1, region >= GRID_W, region < n_region - GRID_W)
    others = (region, region - 1, region + 1, region - GRID_W, region + GRID_W)
    ac, steps = fall.shape[1], fall.shape[2]
    agents, width = cand.shape[2], cand.shape[3]
    tc = steps // chunks
    pieces = chunks * split
    tp = tc // split
    rows = tc * agents
    block = ac * steps
    groups = a_recv.shape[1]
    ga = ac // groups

    barrier = pltpu.get_barrier_semaphore()
    peers = [lax.rem(step + d, ny) for d in range(1, ny)]
    for peer in peers:
        pl.semaphore_signal(barrier, inc=1, device_id=(region, peer), device_id_type=MESH)
    for k in range(1, 5):
        @pl.when(exists[k])
        def _():
            pl.semaphore_signal(barrier, inc=1, device_id=(others[k], step), device_id_type=MESH)

    def own_copy():
        return pltpu.make_async_copy(
            feat.at[pl.ds(pl.multiple_of(step * ac, ac), ac)], fall.at[step], own_sem.at[0]
        )

    def poly_copy():
        return pltpu.make_async_copy(poly, polys.at[0], own_sem.at[1])

    weights = (
        (tw, twv), (sw, swv), (mw, mwv), (fu, fuv), (fd, fdv),
        (nbr_in, nbr), (g1_in, g1), (g2_in, g2), (g3_in, g3), (g4_in, g4),
    )

    def weight_copy(i):
        return pltpu.make_async_copy(weights[i][0], weights[i][1], w_sem.at[i])

    own_copy().start()
    poly_copy().start()
    for i in (5, 6, 0, 2, 1, 3, 4, 7, 8, 9):
        weight_copy(i).start()

    greeted = ny - 1
    for k in range(1, 5):
        greeted = greeted + exists[k].astype(jnp.int32)
    pl.semaphore_wait(barrier, greeted)

    def a_copy(d, g):
        peer = peers[d - 1]
        return pltpu.make_async_remote_copy(
            src_ref=feat.at[pl.ds(peer * ac + g * ga, ga)],
            dst_ref=fall.at[step, pl.ds(g * ga, ga)],
            send_sem=a_send.at[d - 1, g],
            recv_sem=a_recv.at[d - 1, g],
            device_id=(region, peer),
            device_id_type=MESH,
        )

    def p_copy(k):
        return pltpu.make_async_remote_copy(
            src_ref=poly,
            dst_ref=polys.at[OPPOSITE[k]],
            send_sem=p_send.at[k - 1],
            recv_sem=p_recv.at[OPPOSITE[k] - 1],
            device_id=(others[k], step),
            device_id_type=MESH,
        )

    def piece_of(c):
        return pl.ds(c * tp, tp)

    def b_copy(d, c):
        peer = peers[d - 1]
        return pltpu.make_async_remote_copy(
            src_ref=back.at[peer, piece_of(c)],
            dst_ref=cand.at[0, piece_of(c), pl.ds(pl.multiple_of(step * ac, ac), ac)],
            send_sem=b_send.at[d - 1, c],
            recv_sem=b_recv.at[d - 1, c],
            device_id=(region, peer),
            device_id_type=MESH,
        )

    def h_copy(k, c):
        return pltpu.make_async_remote_copy(
            src_ref=cand.at[0, piece_of(c)],
            dst_ref=cand.at[OPPOSITE[k], piece_of(c)],
            send_sem=h_send.at[k - 1, c],
            recv_sem=h_recv.at[OPPOSITE[k] - 1, c],
            device_id=(others[k], step),
            device_id_type=MESH,
        )

    def h_arrival(k, c):
        return pltpu.make_async_remote_copy(
            src_ref=cand.at[0, piece_of(c)],
            dst_ref=cand.at[k, piece_of(c)],
            send_sem=h_send.at[k - 1, c],
            recv_sem=h_recv.at[k - 1, c],
            device_id=(others[k], step),
            device_id_type=MESH,
        )

    def p_arrival(k):
        return pltpu.make_async_remote_copy(
            src_ref=poly,
            dst_ref=polys.at[k],
            send_sem=p_send.at[k - 1],
            recv_sem=p_recv.at[k - 1],
            device_id=(others[k], step),
            device_id_type=MESH,
        )

    for g in range(groups):
        for d in range(1, ny):
            a_copy(d, g).start()
    for k in range(1, 5):
        @pl.when(exists[k])
        def _():
            p_copy(k).start()

    head_rows = (
        lax.broadcasted_iota(jnp.int32, (HEADS, width), 1) // HEAD_DIM
        == lax.broadcasted_iota(jnp.int32, (HEADS, width), 0)
    ).astype(F32)
    row_i = lax.broadcasted_iota(jnp.int32, (block, block), 0)
    col_j = lax.broadcasted_iota(jnp.int32, (block, block), 1)
    to_steps = (col_j == lax.rem(row_i, ac) * steps + row_i // ac).astype(F32).astype(BF16)

    weight_copy(5).wait()
    slot = lax.broadcasted_iota(jnp.int32, (agents, 1), 0)
    ids = jnp.concatenate([other * agents + slot for other in others + (others[0],)], axis=0)
    wide = jnp.concatenate([nbr[...], nbr[...]], axis=1)
    self_id = region * agents + lax.rem(
        lax.broadcasted_iota(jnp.int32, (1, 2 * agents), 1), agents
    )
    linked = jnp.where(self_id == ids, 1.0, 0.0)
    for n in range(nbr.shape[0]):
        linked = jnp.where(wide[n : n + 1] == ids, 1.0, linked)
    bias = jnp.where(linked > 0.5, 0.0, -1e30).T[0:agents, 0 : 5 * agents]

    own_copy().wait()
    weight_copy(0).wait()
    weight_copy(6).wait()

    def one_group(g, carry):
        for d in range(1, ny):
            a_copy(d, g).wait_recv()
        mine = pl.ds(g * ga, ga)
        x = fall[:, mine].reshape(ny * ga * steps, width)
        n1 = normed(x, g1[...])
        q = (dot(n1, twv[0]) * QSCALE).astype(BF16).reshape(ny, ga, steps, width)
        keys = dot(n1, twv[1]).astype(BF16).reshape(ny, ga, steps, width)
        values = dot(n1, twv[2]).astype(BF16).reshape(ny, ga, steps, width)
        every = ny * steps
        mixes = []
        for a in range(ga):
            mixed = small_attention(
                q[:, a].reshape(every, width),
                keys[:, a].reshape(every, width),
                values[:, a].reshape(every, width),
                head_rows,
            )
            mixes.append(mixed.reshape(ny, 1, steps, width))
        o1 = jnp.concatenate(mixes, axis=1).reshape(ny * ga * steps, width)
        after1 = (x.astype(F32) + dot(o1, twv[3])).astype(BF16)
        after[:, mine] = after1.reshape(ny, ga, steps, width)
        return carry

    lax.fori_loop(0, groups, one_group, 0)
    for y in range(ny):
        moved = dot(to_steps, after[y].reshape(block, width))
        back[y] = moved.astype(BF16).reshape(steps, ac, width)

    for c in range(pieces):
        for d in range(1, ny):
            b_copy(d, c).start()

    mine = pltpu.make_async_copy(
        back.at[step], cand.at[0, :, pl.ds(pl.multiple_of(step * ac, ac), ac)], own_sem.at[0]
    )
    mine.start()

    poly_copy().wait()
    weight_copy(2).wait()
    for k in range(1, 5):
        @pl.when(exists[k])
        def _():
            p_arrival(k).wait_recv()

        @pl.when(jnp.logical_not(exists[k]))
        def _():
            polys[k] = polys[0]
            cand[k] = jnp.zeros_like(cand[k])
    count = polys.shape[1]
    for k in range(5):
        here = slice(k * count, (k + 1) * count)
        kp[here] = dot(polys[k], mwv[1]).astype(BF16)
        valid = jnp.float32(1.0) if k == 0 else jnp.where(exists[k], 1.0, 0.0)
        values = (dot(polys[k], mwv[2]) * valid).T.astype(BF16)
        ones = jnp.full((16, count), valid, F32).astype(BF16)
        for h in range(HEADS):
            vext[h, 0:HEAD_DIM, here] = values[h * HEAD_DIM : (h + 1) * HEAD_DIM]
            vext[h, HEAD_DIM : HEAD_DIM + 16, here] = ones

    mine.wait()
    def send_own(c):
        for i in range(split):
            for k in (4, 3, 2, 1):
                @pl.when(exists[k])
                def _():
                    h_copy(k, c * split + i).start()

    def result_copy(c):
        return pltpu.make_async_copy(enc.at[pl.ds(c * tc, tc)], out.at[pl.ds(c * tc, tc)], o_sem.at[c])

    for i in (1, 3, 4, 7, 8, 9):
        weight_copy(i).wait()


    late = ((column == 0) | (column == GRID_W - 1)).astype(jnp.int32)

    def own_part(c, carry):
        for i in range(split):
            for d in range(1, ny):
                b_copy(d, c * split + i).wait_recv()

        @pl.when(c < 2 - late)
        def _():
            send_own(c)

        n2 = normed(cand[0, pl.ds(c * tc, tc)].reshape(rows, width), g2[...])
        keys = dot(n2, swv[1]).astype(BF16)
        values = dot(n2, swv[2]).astype(BF16)
        queries = (dot(n2, swv[0]) * QSCALE).astype(BF16)
        q2[pl.ds(c * tc, tc)] = queries.reshape(tc, agents, width)
        for t in range(tc):
            at = slice(t * agents, (t + 1) * agents)
            found = partial_attention(
                queries[at], keys[at], values[at], head_rows, bias[:, 0:agents]
            )
            for i in range(3):
                own[i, c * tc + t] = found[i]
        return carry

    lax.fori_loop(0, chunks, own_part, 0)

    def one_chunk(c, carry):
        @pl.when((c < chunks - 1) & (late == 1))
        def _():
            send_own(c + 1)

        part = pl.ds(c * tc, tc)
        mixes = []
        for i in range(split):
            for k in range(1, 5):
                @pl.when(exists[k])
                def _():
                    h_arrival(k, c * split + i).wait_recv()

            x = cand[1:5, pl.ds(c * tc + i * tp, tp)].reshape(4 * tp * agents, width)
            n2 = normed(x, g2[...])
            k2[...] = dot(n2, swv[1]).astype(BF16).reshape(4, tp, agents, width)
            v2[...] = dot(n2, swv[2]).astype(BF16).reshape(4, tp, agents, width)
            for t in range(tp):
                at = c * tc + i * tp + t
                num, den, top = partial_attention(
                    q2[at],
                    k2[:, t].reshape(4 * agents, width),
                    v2[:, t].reshape(4 * agents, width),
                    head_rows,
                    bias[:, agents:],
                )
                high = jnp.maximum(top, own[2, at])
                theirs, ours = jnp.exp2(top - high), jnp.exp2(own[2, at] - high)
                num = num * theirs + own[0, at] * ours
                den = den * theirs + own[1, at] * ours
                mixes.append((num / den).astype(BF16))
        o2 = jnp.concatenate(mixes, axis=0)

        @pl.when((c < chunks - 2) & (late == 0))
        def _():
            send_own(c + 2)

        after2 = (cand[0, part].reshape(rows, width).astype(F32) + dot(o2, swv[3])).astype(BF16)
        n3 = normed(after2, g3[...])
        q3 = (dot(n3, mwv[0]) * QSCALE).T.astype(BF16)

        def alone(h):
            own = q3[h * HEAD_DIM : (h + 1) * HEAD_DIM]
            above = [jnp.zeros((h * HEAD_DIM, rows), BF16)] if h > 0 else []
            below = [jnp.zeros((width - (h + 1) * HEAD_DIM, rows), BF16)] if h < HEADS - 1 else []
            return jnp.concatenate(above + [own] + below, axis=0)

        def pair(j):
            return jnp.concatenate([alone(2 * j), alone(2 * j + 1)], axis=1)

        cuts = [slice(i * kp.shape[0] // 1, (i + 1) * kp.shape[0] // 1) for i in range(1)]
        parts = []
        ahead = [dot(kp[cut], pair(0)) for cut in cuts]
        for j in range(HEADS // 2):
            now = ahead
            top = functools.reduce(jnp.maximum, [jnp.max(x, axis=0, keepdims=True) for x in now])
            ahead = []
            sums = [None, None]
            for i, cut in enumerate(cuts):
                if j + 1 < HEADS // 2:
                    ahead.append(dot(kp[cut], pair(j + 1)))
                expo = jnp.exp2(now[i] - top).astype(BF16)
                for e in range(2):
                    term = dot(vext[2 * j + e, :, cut], expo[:, e * rows : (e + 1) * rows])
                    sums[e] = term if sums[e] is None else sums[e] + term
            for both in sums:
                parts.append(both[0:HEAD_DIM] / both[HEAD_DIM : HEAD_DIM + 1])
        o3 = jnp.concatenate(parts, axis=0).T.astype(BF16)
        after3 = (after2.astype(F32) + dot(o3, mwv[3])).astype(BF16)
        n4 = normed(after3, g4[...])
        hidden = jax.nn.gelu(dot(n4, fuv[...]), approximate=True).astype(BF16)
        encoded = (after3.astype(F32) + dot(hidden, fdv[...])).astype(BF16)
        enc[part] = encoded.reshape(tc, agents, width)
        result_copy(c).start()
        return carry

    lax.fori_loop(0, chunks, one_chunk, 0)

    for c in range(chunks):
        result_copy(c).wait()
    for k in range(1, 5):
        @pl.when(exists[k])
        def _():
            p_copy(k).wait_send()
            for c in range(pieces):
                h_copy(k, c).wait_send()

    for c in range(pieces):
        for d in range(1, ny):
            b_copy(d, c).wait_send()
    for g in range(groups):
        for d in range(1, ny):
            a_copy(d, g).wait_send()


def agents_first(x, out):
    steps, agents, width = x.shape
    ac = steps
    block = steps * ac
    row_i = lax.broadcasted_iota(jnp.int32, (block, block), 0)
    col_j = lax.broadcasted_iota(jnp.int32, (block, block), 1)
    to_agents = (col_j == lax.rem(row_i, steps) * ac + row_i // steps).astype(F32).astype(BF16)
    for g in range(agents // ac):
        mine = slice(g * ac, (g + 1) * ac)
        moved = dot(to_agents, x[:, mine].reshape(block, width))
        out[mine] = moved.astype(BF16).reshape(ac, steps, width)


def local(n_region, ny, *args):
    features, neighbours, polylines = args[0:3]
    gains = [g.reshape(1, -1) for g in args[3:7]]
    tw, sw, mw, fu, fd = args[7:12]
    agents, steps, width = features.shape
    ac = agents // ny
    chunks = 4
    tc = steps // chunks
    groups, split = 4, 2
    pieces = chunks * split
    polys = polylines.shape[0]
    anyspace = pl.BlockSpec(memory_space=pl.ANY)
    dma = pltpu.SemaphoreType.DMA
    encoded = pl.pallas_call(
        functools.partial(kernel, n_region, ny, chunks, split),
        out_shape=jax.ShapeDtypeStruct((steps, agents, width), BF16),
        in_specs=[anyspace] * 12,
        out_specs=anyspace,
        scratch_shapes=[
            pltpu.VMEM((ny, ac, steps, width), BF16),
            pltpu.VMEM((ny, ac, steps, width), BF16),
            pltpu.VMEM((ny, steps, ac, width), BF16),
            pltpu.VMEM((5, steps, agents, width), BF16),
            pltpu.VMEM((5, polys, width), BF16),
            pltpu.VMEM((5 * polys, width), BF16),
            pltpu.VMEM((HEADS, HEAD_DIM + 16, 5 * polys), BF16),
            pltpu.VMEM((4, tc // split, agents, width), BF16),
            pltpu.VMEM((4, tc // split, agents, width), BF16),
            pltpu.VMEM((steps, agents, width), BF16),
            pltpu.VMEM((3, steps, agents, width), F32),
            pltpu.VMEM((steps, agents, width), BF16),
            pltpu.VMEM((neighbours.shape[1], agents), jnp.int32),
            pltpu.VMEM((1, width), F32),
            pltpu.VMEM((1, width), F32),
            pltpu.VMEM((1, width), F32),
            pltpu.VMEM((1, width), F32),
            pltpu.VMEM(tw.shape, BF16),
            pltpu.VMEM(sw.shape, BF16),
            pltpu.VMEM(mw.shape, BF16),
            pltpu.VMEM(fu.shape, BF16),
            pltpu.VMEM(fd.shape, BF16),
            dma((2,)),
            dma((10,)),
            dma((chunks,)),
            dma((ny - 1, groups)),
            dma((ny - 1, groups)),
            dma((4,)),
            dma((4,)),
            dma((ny - 1, pieces)),
            dma((ny - 1, pieces)),
            dma((4, pieces)),
            dma((4, pieces)),
        ],
        compiler_params=pltpu.CompilerParams(
            collective_id=0, has_side_effects=True, vmem_limit_bytes=60 * 1024 * 1024
        ),
    )(features, neighbours.T, polylines, *gains, tw, sw, mw, fu, fd)
    return pl.pallas_call(
        agents_first,
        out_shape=jax.ShapeDtypeStruct(features.shape, BF16),
        in_specs=[pl.BlockSpec(memory_space=pltpu.VMEM)],
        out_specs=pl.BlockSpec(memory_space=pltpu.VMEM),
    )(encoded)


def solution(mesh):
    in_specs = (P("region", "step", None), P("region", None), P("region", None)) + (P(),) * 9
    body = functools.partial(local, mesh.shape["region"], mesh.shape["step"])
    return jax.shard_map(
        body, mesh=mesh, in_specs=in_specs, out_specs=P("region", "step", None), check_vma=False
    )
```

```python
import functools
import math

import jax
import jax.numpy as jnp
from jax import lax
from jax.experimental import pallas as pl
from jax.experimental.pallas import tpu as pltpu
from jax.sharding import PartitionSpec as P

HEADS = 8
HEAD_DIM = 32
GRID_W = 4
BF16 = jnp.bfloat16
F32 = jnp.float32
QSCALE = HEAD_DIM ** (-0.5) * math.log2(math.e)
OPPOSITE = (0, 2, 1, 4, 3)
MESH = pl.DeviceIdType.MESH


def dot(a, b):
    return jnp.dot(a, b, preferred_element_type=F32)


def dot_nt(a, b):
    return lax.dot_general(a, b, (((1,), (1,)), ((), ())), preferred_element_type=F32)


def normed(x, gain):
    xf = x.astype(F32)
    inv = lax.rsqrt(jnp.mean(xf * xf, axis=-1, keepdims=True) + 1e-06)
    return (xf * inv * gain).astype(BF16)


def partial_attention(q, keys, values, head_rows, bias=None):
    rows, width = q.shape
    stacked = jnp.concatenate([q * head_rows[h : h + 1].astype(BF16) for h in range(HEADS)], axis=0)
    scores = dot_nt(stacked, keys)
    if bias is not None:
        scores = (scores.reshape(HEADS, rows, -1) + bias[None]).reshape(HEADS * rows, -1)
    top = jnp.max(scores, axis=-1, keepdims=True)
    expo = jnp.exp2(scores - top)
    total = jnp.sum(expo, axis=-1, keepdims=True)
    out = dot(expo.astype(BF16), values)
    picked = [out[0:rows]] + [jnp.broadcast_to(x[0:rows], (rows, width)) for x in (total, top)]
    for h in range(1, HEADS):
        here = head_rows[h : h + 1] > 0.5
        mine = slice(h * rows, (h + 1) * rows)
        picked = [jnp.where(here, x[mine], p) for x, p in zip((out, total, top), picked)]
    return picked


def small_attention(q, keys, values, head_rows):
    num, den, _ = partial_attention(q, keys, values, head_rows)
    return (num / den).astype(BF16)


def kernel(
    n_region, ny, chunks, split,
    feat, nbr_in, poly, g1_in, g2_in, g3_in, g4_in, tw, sw, mw, fu, fd,
    out,
    fall, after, back, cand, polys, kp, vext, k2, v2, q2, own, enc, nbr, g1, g2, g3, g4, twv, swv, mwv, fuv, fdv,
    own_sem, w_sem, o_sem, a_send, a_recv, p_send, p_recv, b_send, b_recv, h_send, h_recv,
):
    region = lax.axis_index("region")
    step = lax.axis_index("step")
    column = lax.rem(region, GRID_W)
    exists = (None, column != 0, column != GRID_W - 1, region >= GRID_W, region < n_region - GRID_W)
    others = (region, region - 1, region + 1, region - GRID_W, region + GRID_W)
    ac, steps = fall.shape[1], fall.shape[2]
    agents, width = cand.shape[2], cand.shape[3]
    tc = steps // chunks
    pieces = chunks * split
    tp = tc // split
    rows = tc * agents
    block = ac * steps
    groups = a_recv.shape[1]
    ga = ac // groups

    barrier = pltpu.get_barrier_semaphore()
    peers = [lax.rem(step + d, ny) for d in range(1, ny)]
    for peer in peers:
        pl.semaphore_signal(barrier, inc=1, device_id=(region, peer), device_id_type=MESH)
    for k in range(1, 5):
        @pl.when(exists[k])
        def _():
            pl.semaphore_signal(barrier, inc=1, device_id=(others[k], step), device_id_type=MESH)

    def own_copy():
        return pltpu.make_async_copy(
            feat.at[pl.ds(pl.multiple_of(step * ac, ac), ac)], fall.at[step], own_sem.at[0]
        )

    def poly_copy():
        return pltpu.make_async_copy(poly, polys.at[0], own_sem.at[1])

    weights = (
        (tw, twv), (sw, swv), (mw, mwv), (fu, fuv), (fd, fdv),
        (nbr_in, nbr), (g1_in, g1), (g2_in, g2), (g3_in, g3), (g4_in, g4),
    )

    def weight_copy(i):
        return pltpu.make_async_copy(weights[i][0], weights[i][1], w_sem.at[i])

    own_copy().start()
    poly_copy().start()
    for i in (5, 6, 0, 2, 1, 3, 4, 7, 8, 9):
        weight_copy(i).start()

    greeted = ny - 1
    for k in range(1, 5):
        greeted = greeted + exists[k].astype(jnp.int32)
    pl.semaphore_wait(barrier, greeted)

    def a_copy(d, g):
        peer = peers[d - 1]
        return pltpu.make_async_remote_copy(
            src_ref=feat.at[pl.ds(peer * ac + g * ga, ga)],
            dst_ref=fall.at[step, pl.ds(g * ga, ga)],
            send_sem=a_send.at[d - 1, g],
            recv_sem=a_recv.at[d - 1, g],
            device_id=(region, peer),
            device_id_type=MESH,
        )

    def p_copy(k):
        return pltpu.make_async_remote_copy(
            src_ref=poly,
            dst_ref=polys.at[OPPOSITE[k]],
            send_sem=p_send.at[k - 1],
            recv_sem=p_recv.at[OPPOSITE[k] - 1],
            device_id=(others[k], step),
            device_id_type=MESH,
        )

    def piece_of(c):
        return pl.ds(c * tp, tp)

    def b_copy(d, c):
        peer = peers[d - 1]
        return pltpu.make_async_remote_copy(
            src_ref=back.at[peer, piece_of(c)],
            dst_ref=cand.at[0, piece_of(c), pl.ds(pl.multiple_of(step * ac, ac), ac)],
            send_sem=b_send.at[d - 1, c],
            recv_sem=b_recv.at[d - 1, c],
            device_id=(region, peer),
            device_id_type=MESH,
        )

    def h_copy(k, c):
        return pltpu.make_async_remote_copy(
            src_ref=cand.at[0, piece_of(c)],
            dst_ref=cand.at[OPPOSITE[k], piece_of(c)],
            send_sem=h_send.at[k - 1, c],
            recv_sem=h_recv.at[OPPOSITE[k] - 1, c],
            device_id=(others[k], step),
            device_id_type=MESH,
        )

    def h_arrival(k, c):
        return pltpu.make_async_remote_copy(
            src_ref=cand.at[0, piece_of(c)],
            dst_ref=cand.at[k, piece_of(c)],
            send_sem=h_send.at[k - 1, c],
            recv_sem=h_recv.at[k - 1, c],
            device_id=(others[k], step),
            device_id_type=MESH,
        )

    def p_arrival(k):
        return pltpu.make_async_remote_copy(
            src_ref=poly,
            dst_ref=polys.at[k],
            send_sem=p_send.at[k - 1],
            recv_sem=p_recv.at[k - 1],
            device_id=(others[k], step),
            device_id_type=MESH,
        )

    for g in range(groups):
        for d in range(1, ny):
            a_copy(d, g).start()
    for k in range(1, 5):
        @pl.when(exists[k])
        def _():
            p_copy(k).start()

    head_rows = (
        lax.broadcasted_iota(jnp.int32, (HEADS, width), 1) // HEAD_DIM
        == lax.broadcasted_iota(jnp.int32, (HEADS, width), 0)
    ).astype(F32)
    row_i = lax.broadcasted_iota(jnp.int32, (block, block), 0)
    col_j = lax.broadcasted_iota(jnp.int32, (block, block), 1)
    to_steps = (col_j == lax.rem(row_i, ac) * steps + row_i // ac).astype(F32).astype(BF16)

    weight_copy(5).wait()
    slot = lax.broadcasted_iota(jnp.int32, (agents, 1), 0)
    ids = jnp.concatenate([other * agents + slot for other in others + (others[0],)], axis=0)
    wide = jnp.concatenate([nbr[...], nbr[...]], axis=1)
    self_id = region * agents + lax.rem(
        lax.broadcasted_iota(jnp.int32, (1, 2 * agents), 1), agents
    )
    linked = jnp.where(self_id == ids, 1.0, 0.0)
    for n in range(nbr.shape[0]):
        linked = jnp.where(wide[n : n + 1] == ids, 1.0, linked)
    bias = jnp.where(linked > 0.5, 0.0, -1e30).T[0:agents, 0 : 5 * agents]

    own_copy().wait()
    weight_copy(0).wait()
    weight_copy(6).wait()

    def one_group(g, carry):
        for d in range(1, ny):
            a_copy(d, g).wait_recv()
        mine = pl.ds(g * ga, ga)
        x = fall[:, mine].reshape(ny * ga * steps, width)
        n1 = normed(x, g1[...])
        q = (dot(n1, twv[0]) * QSCALE).astype(BF16).reshape(ny, ga, steps, width)
        keys = dot(n1, twv[1]).astype(BF16).reshape(ny, ga, steps, width)
        values = dot(n1, twv[2]).astype(BF16).reshape(ny, ga, steps, width)
        every = ny * steps
        mixes = []
        for a in range(ga):
            mixed = small_attention(
                q[:, a].reshape(every, width),
                keys[:, a].reshape(every, width),
                values[:, a].reshape(every, width),
                head_rows,
            )
            mixes.append(mixed.reshape(ny, 1, steps, width))
        o1 = jnp.concatenate(mixes, axis=1).reshape(ny * ga * steps, width)
        after1 = (x.astype(F32) + dot(o1, twv[3])).astype(BF16)
        after[:, mine] = after1.reshape(ny, ga, steps, width)
        return carry

    lax.fori_loop(0, groups, one_group, 0)
    for y in range(ny):
        moved = dot(to_steps, after[y].reshape(block, width))
        back[y] = moved.astype(BF16).reshape(steps, ac, width)

    for c in range(pieces):
        for d in range(1, ny):
            b_copy(d, c).start()

    mine = pltpu.make_async_copy(
        back.at[step], cand.at[0, :, pl.ds(pl.multiple_of(step * ac, ac), ac)], own_sem.at[0]
    )
    mine.start()

    poly_copy().wait()
    weight_copy(2).wait()
    for k in range(1, 5):
        @pl.when(exists[k])
        def _():
            p_arrival(k).wait_recv()

        @pl.when(jnp.logical_not(exists[k]))
        def _():
            polys[k] = polys[0]
            cand[k] = jnp.zeros_like(cand[k])
    count = polys.shape[1]
    for k in range(5):
        here = slice(k * count, (k + 1) * count)
        kp[here] = dot(polys[k], mwv[1]).astype(BF16)
        valid = jnp.float32(1.0) if k == 0 else jnp.where(exists[k], 1.0, 0.0)
        values = (dot(polys[k], mwv[2]) * valid).T.astype(BF16)
        ones = jnp.full((16, count), valid, F32).astype(BF16)
        for h in range(HEADS):
            vext[h, 0:HEAD_DIM, here] = values[h * HEAD_DIM : (h + 1) * HEAD_DIM]
            vext[h, HEAD_DIM : HEAD_DIM + 16, here] = ones

    mine.wait()
    def send_own(c):
        for i in range(split):
            for k in (2, 1, 3, 4):
                @pl.when(exists[k])
                def _():
                    h_copy(k, c * split + i).start()

    def result_copy(c):
        return pltpu.make_async_copy(enc.at[pl.ds(c * tc, tc)], out.at[pl.ds(c * tc, tc)], o_sem.at[c])

    for i in (1, 3, 4, 7, 8, 9):
        weight_copy(i).wait()


    late = ((column == 0) | (column == GRID_W - 1)).astype(jnp.int32)

    def own_part(c, carry):
        for i in range(split):
            for d in range(1, ny):
                b_copy(d, c * split + i).wait_recv()

        @pl.when(c < 2 - late)
        def _():
            send_own(c)

        n2 = normed(cand[0, pl.ds(c * tc, tc)].reshape(rows, width), g2[...])
        keys = dot(n2, swv[1]).astype(BF16)
        values = dot(n2, swv[2]).astype(BF16)
        queries = (dot(n2, swv[0]) * QSCALE).astype(BF16)
        q2[pl.ds(c * tc, tc)] = queries.reshape(tc, agents, width)
        for t in range(tc):
            at = slice(t * agents, (t + 1) * agents)
            found = partial_attention(
                queries[at], keys[at], values[at], head_rows, bias[:, 0:agents]
            )
            for i in range(3):
                own[i, c * tc + t] = found[i]
        return carry

    lax.fori_loop(0, chunks, own_part, 0)

    def one_chunk(c, carry):
        @pl.when((c < chunks - 1) & (late == 1))
        def _():
            send_own(c + 1)

        part = pl.ds(c * tc, tc)
        mixes = []
        for i in range(split):
            for k in range(1, 5):
                @pl.when(exists[k])
                def _():
                    h_arrival(k, c * split + i).wait_recv()

            x = cand[1:5, pl.ds(c * tc + i * tp, tp)].reshape(4 * tp * agents, width)
            n2 = normed(x, g2[...])
            k2[...] = dot(n2, swv[1]).astype(BF16).reshape(4, tp, agents, width)
            v2[...] = dot(n2, swv[2]).astype(BF16).reshape(4, tp, agents, width)
            for t in range(tp):
                at = c * tc + i * tp + t
                num, den, top = partial_attention(
                    q2[at],
                    k2[:, t].reshape(4 * agents, width),
                    v2[:, t].reshape(4 * agents, width),
                    head_rows,
                    bias[:, agents:],
                )
                high = jnp.maximum(top, own[2, at])
                theirs, ours = jnp.exp2(top - high), jnp.exp2(own[2, at] - high)
                num = num * theirs + own[0, at] * ours
                den = den * theirs + own[1, at] * ours
                mixes.append((num / den).astype(BF16))
        o2 = jnp.concatenate(mixes, axis=0)

        @pl.when((c < chunks - 2) & (late == 0))
        def _():
            send_own(c + 2)

        after2 = (cand[0, part].reshape(rows, width).astype(F32) + dot(o2, swv[3])).astype(BF16)
        n3 = normed(after2, g3[...])
        q3 = (dot(n3, mwv[0]) * QSCALE).T.astype(BF16)

        def alone(h):
            own = q3[h * HEAD_DIM : (h + 1) * HEAD_DIM]
            above = [jnp.zeros((h * HEAD_DIM, rows), BF16)] if h > 0 else []
            below = [jnp.zeros((width - (h + 1) * HEAD_DIM, rows), BF16)] if h < HEADS - 1 else []
            return jnp.concatenate(above + [own] + below, axis=0)

        def pair(j):
            return jnp.concatenate([alone(2 * j), alone(2 * j + 1)], axis=1)

        cuts = [slice(i * kp.shape[0] // 1, (i + 1) * kp.shape[0] // 1) for i in range(1)]
        parts = []
        ahead = [dot(kp[cut], pair(0)) for cut in cuts]
        for j in range(HEADS // 2):
            now = ahead
            top = functools.reduce(jnp.maximum, [jnp.max(x, axis=0, keepdims=True) for x in now])
            ahead = []
            sums = [None, None]
            for i, cut in enumerate(cuts):
                if j + 1 < HEADS // 2:
                    ahead.append(dot(kp[cut], pair(j + 1)))
                expo = jnp.exp2(now[i] - top).astype(BF16)
                for e in range(2):
                    term = dot(vext[2 * j + e, :, cut], expo[:, e * rows : (e + 1) * rows])
                    sums[e] = term if sums[e] is None else sums[e] + term
            for both in sums:
                parts.append(both[0:HEAD_DIM] / both[HEAD_DIM : HEAD_DIM + 1])
        o3 = jnp.concatenate(parts, axis=0).T.astype(BF16)
        after3 = (after2.astype(F32) + dot(o3, mwv[3])).astype(BF16)
        n4 = normed(after3, g4[...])
        hidden = jax.nn.gelu(dot(n4, fuv[...]), approximate=True).astype(BF16)
        encoded = (after3.astype(F32) + dot(hidden, fdv[...])).astype(BF16)
        enc[part] = encoded.reshape(tc, agents, width)
        result_copy(c).start()
        return carry

    lax.fori_loop(0, chunks, one_chunk, 0)

    for c in range(chunks):
        result_copy(c).wait()
    for k in range(1, 5):
        @pl.when(exists[k])
        def _():
            p_copy(k).wait_send()
            for c in range(pieces):
                h_copy(k, c).wait_send()

    for c in range(pieces):
        for d in range(1, ny):
            b_copy(d, c).wait_send()
    for g in range(groups):
        for d in range(1, ny):
            a_copy(d, g).wait_send()


def agents_first(x, out):
    steps, agents, width = x.shape
    ac = steps
    block = steps * ac
    row_i = lax.broadcasted_iota(jnp.int32, (block, block), 0)
    col_j = lax.broadcasted_iota(jnp.int32, (block, block), 1)
    to_agents = (col_j == lax.rem(row_i, steps) * ac + row_i // steps).astype(F32).astype(BF16)
    for g in range(agents // ac):
        mine = slice(g * ac, (g + 1) * ac)
        moved = dot(to_agents, x[:, mine].reshape(block, width))
        out[mine] = moved.astype(BF16).reshape(ac, steps, width)


def local(n_region, ny, *args):
    features, neighbours, polylines = args[0:3]
    gains = [g.reshape(1, -1) for g in args[3:7]]
    tw, sw, mw, fu, fd = args[7:12]
    agents, steps, width = features.shape
    ac = agents // ny
    chunks = 4
    tc = steps // chunks
    groups, split = 4, 1
    pieces = chunks * split
    polys = polylines.shape[0]
    anyspace = pl.BlockSpec(memory_space=pl.ANY)
    dma = pltpu.SemaphoreType.DMA
    encoded = pl.pallas_call(
        functools.partial(kernel, n_region, ny, chunks, split),
        out_shape=jax.ShapeDtypeStruct((steps, agents, width), BF16),
        in_specs=[anyspace] * 12,
        out_specs=anyspace,
        scratch_shapes=[
            pltpu.VMEM((ny, ac, steps, width), BF16),
            pltpu.VMEM((ny, ac, steps, width), BF16),
            pltpu.VMEM((ny, steps, ac, width), BF16),
            pltpu.VMEM((5, steps, agents, width), BF16),
            pltpu.VMEM((5, polys, width), BF16),
            pltpu.VMEM((5 * polys, width), BF16),
            pltpu.VMEM((HEADS, HEAD_DIM + 16, 5 * polys), BF16),
            pltpu.VMEM((4, tc // split, agents, width), BF16),
            pltpu.VMEM((4, tc // split, agents, width), BF16),
            pltpu.VMEM((steps, agents, width), BF16),
            pltpu.VMEM((3, steps, agents, width), F32),
            pltpu.VMEM((steps, agents, width), BF16),
            pltpu.VMEM((neighbours.shape[1], agents), jnp.int32),
            pltpu.VMEM((1, width), F32),
            pltpu.VMEM((1, width), F32),
            pltpu.VMEM((1, width), F32),
            pltpu.VMEM((1, width), F32),
            pltpu.VMEM(tw.shape, BF16),
            pltpu.VMEM(sw.shape, BF16),
            pltpu.VMEM(mw.shape, BF16),
            pltpu.VMEM(fu.shape, BF16),
            pltpu.VMEM(fd.shape, BF16),
            dma((2,)),
            dma((10,)),
            dma((chunks,)),
            dma((ny - 1, groups)),
            dma((ny - 1, groups)),
            dma((4,)),
            dma((4,)),
            dma((ny - 1, pieces)),
            dma((ny - 1, pieces)),
            dma((4, pieces)),
            dma((4, pieces)),
        ],
        compiler_params=pltpu.CompilerParams(
            collective_id=0, has_side_effects=True, vmem_limit_bytes=60 * 1024 * 1024
        ),
    )(features, neighbours.T, polylines, *gains, tw, sw, mw, fu, fd)
    return pl.pallas_call(
        agents_first,
        out_shape=jax.ShapeDtypeStruct(features.shape, BF16),
        in_specs=[pl.BlockSpec(memory_space=pltpu.VMEM)],
        out_specs=pl.BlockSpec(memory_space=pltpu.VMEM),
    )(encoded)


def solution(mesh):
    in_specs = (P("region", "step", None), P("region", None), P("region", None)) + (P(),) * 9
    body = functools.partial(local, mesh.shape["region"], mesh.shape["step"])
    return jax.shard_map(
        body, mesh=mesh, in_specs=in_specs, out_specs=P("region", "step", None), check_vma=False
    )
```
